256 devices in a mesh: ty: 8 (over z_hi, x), tx: 32 (over z_lo, y, core).
Axes of the slice: x: 4, y: 4, z: 8 (z_hi: 2, z_lo: 4; z = z_hi * 4 + z_lo), core: 2. Of those that a mesh axis runs over, the one named last changes fastest.
Arguments:
- object_field: float32 [2, 1024, 4096], P(None, 'ty', 'tx'), may hold values from -40 to 40
- probe: float32 [2, 4, 128, 128], replicated, may hold values from -3 to 3
- intensities: float32 [8, 32, 3, 128, 128], P('ty', 'tx'), may hold values from 0.25 to 16
- positions: int32 [8, 32, 3, 2], P('ty', 'tx'), may hold values from 0 to 128
Outputs:
- object_out: float32 [2, 1024, 4096], P(None, 'ty', 'tx')
- probe_out: float32 [2, 4, 128, 128], replicated
The draws below stay inside these ranges and needn't reach their ends.
All inputs are finite; a program needn't handle non-finite values.
Results may differ from the reference program's by a relative error of at most 0.0003.
Values sent between devices are 32-bit elements; how exact they have to be, the bound alone decides.
A program may use at most 64 MiB of HBM per device.

```python
import math
import jax
import jax.numpy as jnp
from jax import lax

WIN = 128
MODES = 4
TILE = 128
SCANS = 3
ROUNDS = 2
NY = 1024
NX = 4096
N_TY = 8
N_TX = 32


def draw_object_field(key, part):
    key_base, key_rows, key_cols = jax.random.split(key, 3)
    row_pos = jnp.arange(NY, dtype=jnp.float32) / NY
    col_pos = jnp.arange(NX, dtype=jnp.float32) / NX
    row_factor = jnp.exp(jax.random.uniform(key_rows, (NY,), jnp.float32, 0.0, jnp.log(3.2)))
    col_factor = jnp.exp(jax.random.uniform(key_cols, (NX,), jnp.float32, 0.0, jnp.log(3.2)))
    base = jnp.clip(jax.random.normal(key_base, (2, NY, NX), jnp.float32), -4.0, 4.0)
    trend = jnp.sqrt(0.5 + row_pos[:, None] + col_pos[None, :])
    scaled = 0.5 * base * trend[None] * row_factor[None, :, None] * col_factor[None, None, :]
    return scaled.astype(jnp.float32)


def place_ends(values, key, least, high):
    shape = values.shape
    spot = [jax.random.randint(jax.random.fold_in(key, axis), (), 0, shape[axis]) for axis in range(len(shape))]
    values = values.at[tuple(spot)].set(least)
    longest = shape.index(max(shape))
    spot[longest] = (spot[longest] + 1) % shape[longest]
    return values.at[tuple(spot)].set(high)


def levels(rng, shape, cuts, smallest, largest):
    gain, own = 1.0, jax.random.fold_in(rng, 6)
    for axis_at, shards_of in cuts:
        draws = jnp.exp(jax.random.uniform(jax.random.fold_in(own, axis_at), (shards_of,), jnp.float32, smallest / len(cuts), largest / len(cuts)))
        gain = gain * jnp.repeat(draws, shape[axis_at] // shards_of).reshape([-1 if axis == axis_at else 1 for axis in range(len(shape))])
    return gain


def scatter_about(stream_key, dims, width, bound, kind=jnp.bfloat16):
    return jnp.clip(width * jax.random.normal(stream_key, dims, jnp.float32), -bound, bound).astype(kind)


def setup_inputs(seed: int = 0) -> dict:
    key_list = jax.random.split(jax.random.key(seed), 5)
    return {
        "object_field": draw_object_field(jax.random.fold_in(key_list[4], 71), 0),
        "probe": scatter_about(key_list[1], (2, MODES, WIN, WIN), 0.5, 3.0, jnp.float32),
        "intensities": jnp.clip(jnp.exp(math.log(16.0) - 4.158883 * jax.random.uniform(key_list[2], (N_TY, N_TX, SCANS, WIN, WIN), jnp.float32) ** levels(key_list[2], (N_TY, N_TX, SCANS, WIN, WIN), ((0, 8), (1, 32)), -0.2, 0.2)), 0.25, 16.0),
        "positions": place_ends(jax.random.randint(key_list[3], (N_TY, N_TX, SCANS, 2), 0, TILE + 1), jax.random.fold_in(key_list[3], 1), 0, TILE).astype(jnp.int32),
    }


OBJECT_STEP = 0.1
PROBE_RELAX = 0.5

def reference(object_field, probe, intensities, positions):
    win_size = probe.shape[-1]
    margin = win_size // 2
    measured = jnp.sqrt(intensities)
    zero_index = jnp.zeros((), jnp.int32)
    for round_index in range(ROUNDS):
        padded = jnp.pad(object_field, ((0, 0), (margin, margin), (margin, margin)))
        probe_cplx = lax.complex(probe[0], probe[1])

        def visit_tile(item_index, loop_state):
            grad_grid, probe_grad, weight = loop_state
            item_int = jnp.asarray(item_index).astype(jnp.int32)
            tile_row = item_int // N_TX
            tile_col = item_int % N_TX
            tile_anchor = jnp.stack([tile_row * TILE, tile_col * TILE]).astype(jnp.int32)
            win_starts = (positions[tile_row, tile_col].astype(jnp.int32) + tile_anchor[None, :]).astype(jnp.int32)

            def cut_window(corner):
                return lax.dynamic_slice(padded, (zero_index, corner[0].astype(jnp.int32), corner[1].astype(jnp.int32)), (2, win_size, win_size))
            windows = jax.vmap(cut_window)(win_starts)
            win_cplx = lax.complex(windows[:, 0], windows[:, 1])
            exit_waves = probe_cplx[None] * win_cplx[:, None]
            far_field = jnp.fft.fft2(exit_waves, norm='ortho')
            far_power = lax.optimization_barrier(jnp.sum(jnp.real(far_field) ** 2 + jnp.imag(far_field) ** 2, axis=1))
            factor = measured[tile_row, tile_col] / jnp.sqrt(jnp.maximum(far_power, 1.0)) - 1.0
            back_field = jnp.fft.ifft2(far_field * factor[:, None], norm='ortho')
            obj_grad = lax.optimization_barrier(jnp.sum(jnp.conj(probe_cplx)[None] * back_field, axis=1))
            probe_grad = probe_grad + lax.optimization_barrier(jnp.sum(jnp.conj(win_cplx)[:, None] * back_field, axis=0))
            weight = weight + jnp.sum(windows * windows)

            def place(scan_index, grid_now):
                corner = win_starts[scan_index]
                start_tuple = (zero_index, corner[0].astype(jnp.int32), corner[1].astype(jnp.int32))
                previous = lax.dynamic_slice(grid_now, start_tuple, (2, win_size, win_size))
                grad_piece = jnp.stack([jnp.real(obj_grad[scan_index]), jnp.imag(obj_grad[scan_index])])
                return lax.dynamic_update_slice(grid_now, previous + grad_piece, start_tuple)
            grad_grid = lax.fori_loop(0, SCANS, place, grad_grid)
            return (grad_grid, probe_grad, weight)
        start_state = (jnp.zeros_like(padded), jnp.zeros_like(probe_cplx), jnp.zeros((), jnp.float32))
        grad_grid, probe_grad, weight = lax.fori_loop(0, N_TY * N_TX, visit_tile, start_state)
        new_object = object_field + OBJECT_STEP * grad_grid[:, margin:-margin, margin:-margin]
        probe_real = jnp.stack([jnp.real(probe_grad), jnp.imag(probe_grad)])
        probe = probe + PROBE_RELAX * win_size * win_size / weight * probe_real
        object_field = new_object
    return (object_field, probe)
```

```python
import functools
import jax
import jax.numpy as jnp
import ml_dtypes
import numpy as np
from jax import lax
from jax.experimental import pallas as pl
from jax.experimental.pallas import tpu as pltpu
from jax.sharding import PartitionSpec as P

ROUNDS = 2
OBJECT_STEP = 0.1
PROBE_RELAX = 0.5
WIN = 128
MODES = 4
SCANS = 3
X, Y, ZH, ZL = 4, 4, 2, 4
HALF = MODES * WIN
MESH = pl.DeviceIdType.MESH
F32, BF16 = jnp.float32, jnp.bfloat16


def dft_tables():
    line = np.arange(WIN)
    angle = (line[:, None] * line[None, :] % WIN) * (2.0 * np.pi / WIN)
    c, s = np.cos(angle) * WIN**-0.5, np.sin(angle) * WIN**-0.5
    a = np.block([[c, -s], [s, c]])
    parts = []
    for m in (a, a.T):
        hi = m.astype(ml_dtypes.bfloat16)
        lo = (m - hi.astype(np.float64)).astype(ml_dtypes.bfloat16)
        parts += [hi, lo]
    return np.stack(parts)


def split(x):
    hi = x.astype(BF16)
    return hi, (x - hi.astype(F32)).astype(BF16)


def mm(a, b):
    return jnp.dot(a, b, preferred_element_type=F32)


def kernel(
    obj, probe, inten, pos, tab, obj_out, probe_out,
    ext, zp, gq, lrb, eb, udb, pk, hlr, hud, hco, xh, xl, uf, win, pg, wacc,
    crb, hs, rxb, zbuf, pn, wcb, w1, wxb, wzb,
    halo_s, halo_r, lr_s, lr_r, ud_s, ud_r, co_s, co_r, xy_s, xy_r, z_s, z_r, ag_s, ag_r, fw_s, fw_r,
):
    ty, tx = lax.axis_index("ty"), lax.axis_index("tx")
    nty, ntx = ZH * X, ZL * Y * 2
    zh, x = ty // X, ty % X
    zl, y, core = tx // (2 * Y), (tx // 2) % Y, tx % 2
    z = zh * ZL + zl
    q = x * Y + y
    piece = HALF // (X * Y)
    nz = ZH * ZL

    up, down = (ty + nty - 1) % nty, (ty + 1) % nty
    left, right = (tx + ntx - 1) % ntx, (tx + 1) % ntx
    has_up, has_down = ty > 0, ty < nty - 1
    has_left, has_right = tx > 0, tx < ntx - 1
    partner = (ty, tx + 1 - 2 * core)

    def xy_peer(d):
        px, py = (x + d // Y) % X, (y + d % Y) % Y
        return (zh * X + px, zl * 2 * Y + py * 2 + core), px * Y + py

    def z_peer(d):
        pz = (z + d) % nz
        return ((pz // ZL) * X + x, (pz % ZL) * 2 * Y + y * 2 + core)

    def remote(src, dst, ssem, rsem, device):
        return pltpu.make_async_remote_copy(
            src_ref=src, dst_ref=dst, send_sem=ssem, recv_sem=rsem, device_id=device, device_id_type=MESH
        )

    lane = lax.broadcasted_iota(jnp.int32, (WIN, WIN), 1)
    low = lane < 64
    o_re, o_im = obj[0], obj[1]
    r_re, r_im = pltpu.roll(o_re, 64, 1), pltpu.roll(o_im, 64, 1)
    pk[0] = jnp.where(low, o_re, r_im)
    pk[1] = jnp.where(low, r_re, o_im)

    peers = [partner, (ty, left), (ty, right), (up, tx), (down, tx), (up, left), (up, right), (down, left), (down, right)]
    peers += [xy_peer(d)[0] for d in range(1, X * Y)] + [z_peer(d) for d in range(1, nz)]
    barrier = pltpu.get_barrier_semaphore()
    for peer in peers:
        pl.semaphore_signal(barrier, inc=1, device_id=peer, device_id_type=MESH)
    zp[...] = jnp.zeros_like(zp)
    pl.semaphore_wait(barrier, len(peers))

    top, bottom = pl.ds(0, 64), pl.ds(64, 64)
    halo = [
        (obj.at[:, bottom, :], hud.at[0], (down, tx)),
        (obj.at[:, top, :], hud.at[1], (up, tx)),
        (pk.at[1], hlr.at[0], (ty, right)),
        (pk.at[0], hlr.at[1], (ty, left)),
        (pk.at[1, bottom, :], hco.at[0], (down, right)),
        (pk.at[0, bottom, :], hco.at[1], (down, left)),
        (pk.at[1, top, :], hco.at[2], (up, right)),
        (pk.at[0, top, :], hco.at[3], (up, left)),
    ]
    halo = [remote(s, d, halo_s.at[i], halo_r.at[i], p) for i, (s, d, p) in enumerate(halo)]
    for copy in halo:
        copy.start()
    for copy in halo:
        copy.wait_recv()
    zero = jnp.float32(0.0)

    def extend(rows, mid_re, mid_im, from_left, from_right, keep):
        n = mid_re.shape[0]
        low_n = low[:n]
        keep_l = jnp.where(keep & has_left, 1.0, 0.0)
        keep_r = jnp.where(keep & has_right, 1.0, 0.0)
        keep_m = jnp.where(keep, 1.0, 0.0)
        m_re, m_im = pltpu.roll(mid_re, 64, 1) * keep_m, pltpu.roll(mid_im, 64, 1) * keep_m
        fl, fr = from_left * keep_l, from_right * keep_r
        ext[0, 0, rows, :] = jnp.where(low_n, fl, m_re)
        ext[0, 1, rows, :] = jnp.where(low_n, pltpu.roll(fl, 64, 1), m_im)
        ext[1, 0, rows, :] = jnp.where(low_n, m_re, pltpu.roll(fr, 64, 1))
        ext[1, 1, rows, :] = jnp.where(low_n, m_im, fr)

    extend(pl.ds(64, 128), obj[0], obj[1], hlr[0], hlr[1], True)
    extend(pl.ds(0, 64), hud[0, 0], hud[0, 1], hco[0], hco[1], has_up)
    extend(pl.ds(192, 64), hud[1, 0], hud[1, 1], hco[2], hco[3], has_down)

    for rnd in range(ROUNDS):
        probe_now = probe if rnd == 0 else pn.at[rnd - 1]
        gq[rnd] = jnp.zeros_like(gq.at[rnd])
        pg[rnd] = jnp.zeros_like(pg.at[rnd])
        wacc[rnd] = jnp.zeros_like(wacc.at[rnd])

        def scan(s, carry):
            r, c = pos[s, 0], pos[s, 1]
            back = (WIN - c) & (WIN - 1)
            first = lane + c < WIN
            w = wacc[rnd]
            for comp in range(2):
                x0 = pltpu.roll(ext[0, comp, pl.ds(r, WIN), :], back, 1)
                x1 = pltpu.roll(ext[1, comp, pl.ds(r, WIN), :], back, 1)
                o = jnp.where(first, x0, x1)
                win[comp] = o
                w = w + jnp.sum((o * o).reshape(WIN // 8, 8, WIN), axis=0)
            wacc[rnd] = w
            w_re, w_im = win[0], win[1]
            for k in range(MODES):
                cols = slice(k * WIN, (k + 1) * WIN)
                p_re, p_im = probe_now[cols, :], probe_now[HALF + k * WIN : HALF + (k + 1) * WIN, :]
                xh[0:WIN, cols], xl[0:WIN, cols] = split(p_re * w_re - p_im * w_im)
                xh[WIN:, cols], xl[WIN:, cols] = split(p_re * w_im + p_im * w_re)
            power = jnp.zeros((WIN, WIN), F32)
            for j in range(MODES // 2):
                cols = slice(j * 256, (j + 1) * 256)
                t = mm(tab[2], xh[:, cols]) + mm(tab[2], xl[:, cols]) + mm(tab[3], xh[:, cols])
                for i in range(2):
                    k = 2 * j + i
                    yt = jnp.concatenate([t[0:WIN, i * WIN : (i + 1) * WIN], t[WIN:, i * WIN : (i + 1) * WIN]], axis=1)
                    yh, yl = split(yt)
                    u = mm(yh, tab[0]) + mm(yl, tab[0]) + mm(yh, tab[1])
                    uf[k] = u
                    power = power + u[:, 0:WIN] * u[:, 0:WIN] + u[:, WIN:] * u[:, WIN:]
            factor = jnp.sqrt(inten[s]) / jnp.sqrt(jnp.maximum(power, 1.0)) - 1.0
            factor = jnp.concatenate([factor, factor], axis=1)
            for k in range(MODES):
                cols = slice(k * WIN, (k + 1) * WIN)
                vh, vl = split(uf[k] * factor)
                b = mm(vh, tab[2]) + mm(vl, tab[2]) + mm(vh, tab[3])
                xh[0:WIN, cols], xl[0:WIN, cols] = split(b[:, 0:WIN])
                xh[WIN:, cols], xl[WIN:, cols] = split(b[:, WIN:])
            g_re = jnp.zeros((WIN, WIN), F32)
            g_im = jnp.zeros((WIN, WIN), F32)
            for j in range(MODES // 2):
                cols = slice(j * 256, (j + 1) * 256)
                b = mm(tab[0], xh[:, cols]) + mm(tab[0], xl[:, cols]) + mm(tab[1], xh[:, cols])
                for i in range(2):
                    k = 2 * j + i
                    b_re, b_im = b[0:WIN, i * WIN : (i + 1) * WIN], b[WIN:, i * WIN : (i + 1) * WIN]
                    re_rows = slice(k * WIN, (k + 1) * WIN)
                    im_rows = slice(HALF + k * WIN, HALF + (k + 1) * WIN)
                    p_re, p_im = probe_now[re_rows, :], probe_now[im_rows, :]
                    g_re = g_re + p_re * b_re + p_im * b_im
                    g_im = g_im + p_re * b_im - p_im * b_re
                    w_re, w_im = win[0], win[1]
                    pg[rnd, re_rows, :] += w_re * b_re + w_im * b_im
                    pg[rnd, im_rows, :] += w_re * b_im - w_im * b_re
            turn = c & (WIN - 1)
            inside = lane >= c
            for comp, g in enumerate((g_re, g_im)):
                g = pltpu.roll(g, turn, 1)
                zp[0, comp, WIN : 2 * WIN, :] = jnp.where(inside, g, 0.0)
                zp[1, comp, WIN : 2 * WIN, :] = jnp.where(inside, 0.0, g)
            for half in range(2):
                for comp in range(2):
                    gq[rnd, half, comp] += zp[half, comp, pl.ds(WIN - r, 2 * WIN), :]
            return carry

        lax.fori_loop(0, SCANS, scan, 0)

        mine = pl.multiple_of(core * HALF, HALF)
        theirs = pl.multiple_of((1 - core) * HALF, HALF)
        core_copies = [
            remote(wacc.at[rnd], wcb.at[rnd], co_s.at[rnd, 0], co_r.at[rnd, 0], partner),
            remote(pg.at[rnd, pl.ds(theirs, HALF), :], crb.at[rnd], co_s.at[rnd, 1], co_r.at[rnd, 1], partner),
        ]
        for copy in core_copies:
            copy.start()
        lr = [
            remote(gq.at[rnd, 1], lrb.at[rnd, 0], lr_s.at[rnd, 0], lr_r.at[rnd, 0], (ty, right)),
            remote(gq.at[rnd, 0], lrb.at[rnd, 1], lr_s.at[rnd, 1], lr_r.at[rnd, 1], (ty, left)),
        ]
        for copy in lr:
            copy.start()
        for copy in core_copies:
            copy.wait_recv()
        hs[rnd] = pg[rnd, pl.ds(mine, HALF), :] + crb[rnd]
        w_pair = wacc[rnd] + wcb[rnd]
        w1[rnd, 0] = w_pair
        xy = []
        for d in range(1, X * Y):
            device, pq = xy_peer(d)
            rows = pl.ds(pl.multiple_of(pq * piece, piece), piece)
            xy.append(remote(hs.at[rnd, rows, :], rxb.at[rnd, q], xy_s.at[rnd, 0, d], xy_r.at[rnd, 0, d], device))
            xy.append(remote(w1.at[rnd, 0], wxb.at[rnd, q], xy_s.at[rnd, 1, d], xy_r.at[rnd, 1, d], device))
        for copy in xy:
            copy.start()
        for copy in lr:
            copy.wait_recv()
        eb[rnd, 0] = gq[rnd, 0] + jnp.where(has_left, lrb[rnd, 0], 0.0)
        eb[rnd, 1] = gq[rnd, 1] + jnp.where(has_right, lrb[rnd, 1], 0.0)
        ud = [
            remote(eb.at[rnd, :, :, pl.ds(128, 128), :], udb.at[rnd, 0], ud_s.at[rnd, 0], ud_r.at[rnd, 0], (down, tx)),
            remote(eb.at[rnd, :, :, pl.ds(0, 128), :], udb.at[rnd, 1], ud_s.at[rnd, 1], ud_r.at[rnd, 1], (up, tx)),
        ]
        for copy in ud:
            copy.start()
        own = pl.ds(pl.multiple_of(q * piece, piece), piece)
        rxb[rnd, q] = hs[rnd, own, :]
        wxb[rnd, q] = w_pair
        for copy in xy:
            copy.wait_recv()
        total, w_total = rxb[rnd, 0], wxb[rnd, 0]
        for i in range(1, X * Y):
            total, w_total = total + rxb[rnd, i], w_total + wxb[rnd, i]
        zbuf[rnd, z] = total
        wzb[rnd, z] = w_total
        zc = []
        for d in range(1, nz):
            device = z_peer(d)
            zc.append(remote(zbuf.at[rnd, z], zbuf.at[rnd, z], z_s.at[rnd, 0, d], z_r.at[rnd, 0, d], device))
            zc.append(remote(wzb.at[rnd, z], wzb.at[rnd, z], z_s.at[rnd, 1, d], z_r.at[rnd, 1, d], device))
        for copy in zc:
            copy.start()
        for copy in ud:
            copy.wait_recv()
        for half in range(2):
            in_cols = (lane >= 64) | has_left if half == 0 else (lane < 64) | has_right
            for row in range(2):
                rows = pl.ds(row * 128, 128)
                sub = lax.broadcasted_iota(jnp.int32, (WIN, WIN), 0)
                in_rows = (sub >= 64) | has_up if row == 0 else (sub < 64) | has_down
                there = has_up if row == 0 else has_down
                for comp in range(2):
                    add = eb[rnd, half, comp, rows, :] + jnp.where(there, udb[rnd, row, half, comp], 0.0)
                    ext[half, comp, rows, :] += jnp.where(in_cols & in_rows, OBJECT_STEP * add, 0.0)
        if rnd == ROUNDS - 1:
            for comp in range(2):
                a, b = ext[0, comp, 64:192, :], ext[1, comp, 64:192, :]
                obj_out[comp] = jnp.where(low, pltpu.roll(a, 64, 1), pltpu.roll(b, 64, 1))
        for copy in zc:
            copy.wait_recv()
        total, w_total = zbuf[rnd, 0], wzb[rnd, 0]
        for i in range(1, nz):
            total, w_total = total + zbuf[rnd, i], w_total + wzb[rnd, i]
        weight = jnp.sum(w_total, axis=(0, 1), keepdims=True)
        place = pl.ds(pl.multiple_of(core * HALF + q * piece, piece), piece)
        pn[rnd, place, :] = probe_now[place, :] + PROBE_RELAX * WIN * WIN / weight * total
        ag = []
        for d in range(1, X * Y):
            device, _ = xy_peer(d)
            ag.append(remote(pn.at[rnd, place, :], pn.at[rnd, place, :], ag_s.at[rnd, d], ag_r.at[rnd, d], device))
        for copy in ag:
            copy.start()
        fw = [remote(pn.at[rnd, place, :], pn.at[rnd, place, :], fw_s.at[rnd, 0], fw_r.at[rnd, 0], partner)]
        fw[0].start()
        for d in range(1, X * Y):
            ag[d - 1].wait_recv()
            source = ((x + X - d // Y) % X) * Y + (y + Y - d % Y) % Y
            rows = pl.ds(pl.multiple_of(core * HALF + source * piece, piece), piece)
            fw.append(remote(pn.at[rnd, rows, :], pn.at[rnd, rows, :], fw_s.at[rnd, d], fw_r.at[rnd, d], partner))
            fw[d].start()
        for copy in fw:
            copy.wait_recv()
        for copy in core_copies + lr + xy + ud + zc + ag + fw:
            copy.wait_send()
    for copy in halo:
        copy.wait_send()
    probe_out[...] = pn[ROUNDS - 1]


def per_device(object_field, probe, intensities, positions):
    nq, nz = X * Y, ZH * ZL
    piece = HALF // nq
    vmem = lambda *shape, dtype=F32: pltpu.VMEM(shape, dtype)
    dma = lambda *shape: pltpu.SemaphoreType.DMA(shape)
    r = ROUNDS
    full = pl.BlockSpec(memory_space=pltpu.VMEM)
    obj, new_probe = pl.pallas_call(
        kernel,
        out_shape=(
            jax.ShapeDtypeStruct((2, WIN, WIN), F32),
            jax.ShapeDtypeStruct((2 * HALF, WIN), F32),
        ),
        in_specs=[full, full, full, pl.BlockSpec(memory_space=pltpu.SMEM), full],
        out_specs=(full, full),
        scratch_shapes=[
            vmem(2, 2, 256, 128),
            vmem(2, 2, 384, 128),
            vmem(r, 2, 2, 256, 128),
            vmem(r, 2, 2, 256, 128),
            vmem(r, 2, 2, 256, 128),
            vmem(r, 2, 2, 2, 128, 128),
            vmem(2, 128, 128),
            vmem(2, 128, 128),
            vmem(2, 2, 64, 128),
            vmem(4, 64, 128),
            vmem(256, 512, dtype=BF16),
            vmem(256, 512, dtype=BF16),
            vmem(MODES, 128, 256),
            vmem(2, 128, 128),
            vmem(r, 2 * HALF, 128),
            vmem(r, 8, 128),
            vmem(r, HALF, 128),
            vmem(r, HALF, 128),
            vmem(r, nq, piece, 128),
            vmem(r, nz, piece, 128),
            vmem(r, 2 * HALF, 128),
            vmem(r, 8, 128),
            vmem(r, 1, 8, 128),
            vmem(r, nq, 8, 128),
            vmem(r, nz, 8, 128),
            dma(8), dma(8),
            dma(r, 2), dma(r, 2),
            dma(r, 2), dma(r, 2),
            dma(r, 2), dma(r, 2),
            dma(r, 2, nq), dma(r, 2, nq),
            dma(r, 2, nz), dma(r, 2, nz),
            dma(r, nq), dma(r, nq),
            dma(r, nq), dma(r, nq),
        ],
        compiler_params=pltpu.CompilerParams(
            collective_id=0, has_side_effects=True, vmem_limit_bytes=48 * 1024 * 1024
        ),
    )(
        object_field,
        probe.reshape(2 * HALF, WIN),
        intensities.reshape(SCANS, WIN, WIN),
        positions.reshape(SCANS, 2),
        jnp.asarray(dft_tables()),
    )
    return obj, new_probe.reshape(2, MODES, WIN, WIN)


def solution(mesh):
    placed = (P(None, "ty", "tx"), P(), P("ty", "tx", None, None, None), P("ty", "tx", None, None))
    return jax.shard_map(
        per_device,
        mesh=mesh,
        in_specs=placed,
        out_specs=(P(None, "ty", "tx"), P()),
        check_vma=False,
    )
```

```python
import jax
import jax.numpy as jnp
import ml_dtypes
import numpy as np
from jax import lax
from jax.experimental import pallas as pl
from jax.experimental.pallas import tpu as pltpu
from jax.sharding import PartitionSpec as P

ROUNDS = 2
OBJECT_STEP = 0.1
PROBE_RELAX = 0.5
WIN = 128
MODES = 4
SCANS = 3
PAIRS = MODES // 2
X, Y, ZH, ZL = 4, 4, 2, 4
HALF = MODES * WIN
CHUNK = HALF // PAIRS
MESH = pl.DeviceIdType.MESH
F32, BF16 = jnp.float32, jnp.bfloat16


def dft_tables():
    line = np.arange(WIN)
    angle = (line[:, None] * line[None, :] % WIN) * (2.0 * np.pi / WIN)
    c, s = np.cos(angle) * WIN**-0.5, np.sin(angle) * WIN**-0.5
    a = np.block([[c, -s], [s, c]])
    parts = []
    for m in (a, a.T):
        hi = m.astype(ml_dtypes.bfloat16)
        lo = (m - hi.astype(np.float64)).astype(ml_dtypes.bfloat16)
        parts += [hi, lo]
    return np.stack(parts)


def split(x):
    hi = x.astype(BF16)
    return hi, (x - hi.astype(F32)).astype(BF16)


def mm(a, b):
    return jnp.dot(a, b, preferred_element_type=F32)


def left_mm(tab, i, x):
    hi, lo = split(x)
    return mm(tab[i], hi) + mm(tab[i], lo) + mm(tab[i + 1], hi)


def right_mm(x, tab, i):
    hi, lo = split(x)
    return mm(hi, tab[i]) + mm(lo, tab[i]) + mm(hi, tab[i + 1])


def regroup(t):
    top = jnp.concatenate([t[:WIN, :WIN], t[WIN:, :WIN]], axis=1)
    bottom = jnp.concatenate([t[:WIN, WIN:], t[WIN:, WIN:]], axis=1)
    return jnp.concatenate([top, bottom], axis=0)


def kernel(
    obj_hbm, probe_hbm, inten_hbm, pos, tab_hbm, obj_out, probe_out,
    probe, inten, tab, objm, hlr, pk, ext, zp, gq, lrp, lrb, mb, udb, uf, pw, win, gs, pg, wacc,
    crb, wcb, hs, rxb, zbuf, pn,
    in_s, halo_s, halo_r, lr_s, lr_r, ud_s, ud_r, co_s, co_r, xy_s, xy_r, z_s, z_r, ag_s, ag_r, fw_s, fw_r,
):
    ty, tx = lax.axis_index("ty"), lax.axis_index("tx")
    nty, ntx = ZH * X, ZL * Y * 2
    zh, x = ty // X, ty % X
    zl, y, core = tx // (2 * Y), (tx // 2) % Y, tx % 2
    z = zh * ZL + zl
    q = x * Y + y
    piece = CHUNK // (X * Y)
    nz = ZH * ZL

    has_up, has_down = ty > 0, ty < nty - 1
    has_left, has_right = tx > 0, tx < ntx - 1
    up, down = (ty + nty - 1) % nty, (ty + 1) % nty
    left, right = (tx + ntx - 1) % ntx, (tx + 1) % ntx
    partner = (ty, tx + 1 - 2 * core)

    def xy_peer(d):
        px, py = (x + d // Y) % X, (y + d % Y) % Y
        return (zh * X + px, zl * 2 * Y + py * 2 + core), px * Y + py

    def z_peer(d):
        pz = (z + d) % nz
        return ((pz // ZL) * X + x, (pz % ZL) * 2 * Y + y * 2 + core)

    def remote(src, dst, ssem, rsem, device):
        return pltpu.make_async_remote_copy(
            src_ref=src, dst_ref=dst, send_sem=ssem, recv_sem=rsem, device_id=device, device_id_type=MESH
        )

    loads = [
        pltpu.make_async_copy(obj_hbm, objm.at[0, :, pl.ds(64, WIN), :], in_s.at[0]),
        pltpu.make_async_copy(probe_hbm, probe, in_s.at[1]),
        pltpu.make_async_copy(tab_hbm, tab, in_s.at[2]),
        pltpu.make_async_copy(inten_hbm, inten, in_s.at[3]),
    ]
    for copy in loads:
        copy.start()
    peers = [partner, (ty, left), (ty, right), (up, tx), (down, tx), (up, left), (up, right), (down, left), (down, right)]
    peers += [xy_peer(d)[0] for d in range(1, X * Y)] + [z_peer(d) for d in range(1, nz)]
    barrier = pltpu.get_barrier_semaphore()
    for peer in peers:
        pl.semaphore_signal(barrier, inc=1, device_id=peer, device_id_type=MESH)

    low = lax.broadcasted_iota(jnp.int32, (WIN, WIN), 1) < 64
    lane = lax.broadcasted_iota(jnp.int32, (WIN, WIN), 1)
    low2 = lax.broadcasted_iota(jnp.int32, (2 * WIN, WIN), 1) < 64
    zp[...] = jnp.zeros_like(zp)
    loads[0].wait()

    def pack(re, im, low):
        return jnp.where(low, re, pltpu.roll(im, 64, 1)), jnp.where(low, pltpu.roll(re, 64, 1), im)

    pk[0, 0, 64:192, :], pk[0, 1, 64:192, :] = pack(objm[0, 0, 64:192, :], objm[0, 1, 64:192, :], low)

    @pl.when(jnp.logical_not(has_left))
    def _():
        hlr[:, 0] = jnp.zeros_like(hlr.at[:, 0])
        lrb[:, 0] = jnp.zeros_like(lrb.at[:, 0])

    @pl.when(jnp.logical_not(has_right))
    def _():
        hlr[:, 1] = jnp.zeros_like(hlr.at[:, 1])
        lrb[:, 1] = jnp.zeros_like(lrb.at[:, 1])

    @pl.when(jnp.logical_not(has_up))
    def _():
        hlr[0, :, 0:64, :] = jnp.zeros((2, 64, WIN), F32)
        objm[0, :, 0:64, :] = jnp.zeros((2, 64, WIN), F32)
        udb[:, 0] = jnp.zeros_like(udb.at[:, 0])

    @pl.when(jnp.logical_not(has_down))
    def _():
        hlr[0, :, 192:256, :] = jnp.zeros((2, 64, WIN), F32)
        objm[0, :, 192:256, :] = jnp.zeros((2, 64, WIN), F32)
        udb[:, 1] = jnp.zeros_like(udb.at[:, 1])

    pl.semaphore_wait(barrier, len(peers))

    def start(copies):
        for copy, to, _ in copies:
            @pl.when(to)
            def _():
                copy.start()

    def wait_recv(copies):
        for copy, _, came in copies:
            @pl.when(came)
            def _():
                copy.wait_recv()

    def wait_send(copies):
        for copy, to, _ in copies:
            @pl.when(to)
            def _():
                copy.wait_send()

    top, bottom, mid = pl.ds(64, 64), pl.ds(128, 64), pl.ds(64, 128)
    above, below = pl.ds(0, 64), pl.ds(192, 64)
    halo = [
        (objm.at[0, :, bottom, :], objm.at[0, :, above, :], (down, tx), has_down, has_up),
        (objm.at[0, :, top, :], objm.at[0, :, below, :], (up, tx), has_up, has_down),
        (pk.at[0, 1, mid, :], hlr.at[0, 0, mid, :], (ty, right), has_right, has_left),
        (pk.at[0, 0, mid, :], hlr.at[0, 1, mid, :], (ty, left), has_left, has_right),
        (pk.at[0, 1, bottom, :], hlr.at[0, 0, above, :], (down, right), has_down & has_right, has_up & has_left),
        (pk.at[0, 0, bottom, :], hlr.at[0, 1, above, :], (down, left), has_down & has_left, has_up & has_right),
        (pk.at[0, 1, top, :], hlr.at[0, 0, below, :], (up, right), has_up & has_right, has_down & has_left),
        (pk.at[0, 0, top, :], hlr.at[0, 1, below, :], (up, left), has_up & has_left, has_down & has_right),
    ]
    halo = [(remote(s, d, halo_s.at[i], halo_r.at[i], p), to, came) for i, (s, d, p, to, came) in enumerate(halo)]
    start(halo)
    for copy in loads[1:]:
        copy.wait()
    sent = [halo]
    wait_recv(halo)

    def windows(rnd):
        m_re, m_im = pltpu.roll(objm[rnd, 0], 64, 1), pltpu.roll(objm[rnd, 1], 64, 1)
        fl, fr = hlr[rnd, 0], hlr[rnd, 1]
        ext[0, 0] = jnp.where(low2, fl, m_re)
        ext[0, 1] = jnp.where(low2, pltpu.roll(fl, 64, 1), m_im)
        ext[1, 0] = jnp.where(low2, m_re, pltpu.roll(fr, 64, 1))
        ext[1, 1] = jnp.where(low2, m_im, fr)
        wacc[rnd] = jnp.zeros_like(wacc.at[rnd])
        gq[rnd] = jnp.zeros_like(gq.at[rnd])
        pg[rnd] = jnp.zeros_like(pg.at[rnd])

        def cut(s, carry):
            r, c = pos[s, 0], pos[s, 1]
            back = (WIN - c) & (WIN - 1)
            first = lane + c < WIN
            w = wacc[rnd]
            for comp in range(2):
                x0 = pltpu.roll(ext[0, comp, pl.ds(r, WIN), :], back, 1)
                x1 = pltpu.roll(ext[1, comp, pl.ds(r, WIN), :], back, 1)
                o = jnp.where(first, x0, x1)
                win[s, comp] = o
                w = w + jnp.sum((o * o).reshape(WIN // 8, 8, WIN), axis=0)
            wacc[rnd] = w
            return carry

        lax.fori_loop(0, SCANS, cut, 0, unroll=True)

    def modes_of(ref, j):
        return [
            (ref[k * WIN : (k + 1) * WIN, :], ref[HALF + k * WIN : HALF + (k + 1) * WIN, :])
            for k in range(2 * j, 2 * j + 2)
        ]

    def forward(probe_now, j):
        def step(s, carry):
            w_re, w_im = win[s, 0], win[s, 1]
            (a_re, a_im), (b_re, b_im) = modes_of(probe_now, j)
            wave_re = jnp.concatenate([a_re * w_re - a_im * w_im, b_re * w_re - b_im * w_im], axis=1)
            wave_im = jnp.concatenate([a_re * w_im + a_im * w_re, b_re * w_im + b_im * w_re], axis=1)
            t = left_mm(tab, 2, jnp.concatenate([wave_re, wave_im], axis=0))
            u = right_mm(regroup(t), tab, 0)
            uf[s, j] = u
            u2 = u * u
            p = (u2[:WIN, :WIN] + u2[:WIN, WIN:]) + (u2[WIN:, :WIN] + u2[WIN:, WIN:])
            if j == 0:
                pw[s] = p
            else:
                p = pw[s] + p
                pw[s] = jnp.sqrt(inten[s]) / jnp.sqrt(jnp.maximum(p, 1.0)) - 1.0
            return carry

        lax.fori_loop(0, SCANS, step, 0, unroll=True)

    def backward(rnd, probe_now, j, lo, hi):
        def step(s, carry):
            f = jnp.concatenate([pw[s], pw[s]], axis=1)
            b = right_mm(uf[s, j] * jnp.concatenate([f, f], axis=0), tab, 2)
            t = left_mm(tab, 0, regroup(b))
            w_re, w_im = win[s, 0], win[s, 1]
            g_re, g_im = (0.0, 0.0) if j == 0 else (gs[s, 0], gs[s, 1])
            for i, (p_re, p_im) in enumerate(modes_of(probe_now, j)):
                k = 2 * j + i
                b_re, b_im = t[:WIN, i * WIN : (i + 1) * WIN], t[WIN:, i * WIN : (i + 1) * WIN]
                g_re = g_re + p_re * b_re + p_im * b_im
                g_im = g_im + p_re * b_im - p_im * b_re
                pg[rnd, k * WIN : (k + 1) * WIN, :] += w_re * b_re + w_im * b_im
                pg[rnd, HALF + k * WIN : HALF + (k + 1) * WIN, :] += w_re * b_im - w_im * b_re
            if j < PAIRS - 1:
                gs[s, 0], gs[s, 1] = g_re, g_im
            else:
                r, c = pos[s, 0], pos[s, 1]
                turn = c & (WIN - 1)
                inside = lane >= c
                for comp, g in enumerate((g_re, g_im)):
                    g = pltpu.roll(g, turn, 1)
                    zp[0, comp, WIN : 2 * WIN, :] = jnp.where(inside, g, 0.0)
                    zp[1, comp, WIN : 2 * WIN, :] = jnp.where(inside, 0.0, g)
                for half in range(2):
                    for comp in range(2):
                        gq[rnd, half, comp] += zp[half, comp, pl.ds(WIN - r, 2 * WIN), :]
            return carry

        lax.fori_loop(lo, hi, step, 0, unroll=True)

    def all_reduce(rnd, probe_now, j):
        rows = piece + (8 if j == 0 else 0)
        n = pl.ds(0, rows)
        copies = []

        def go(new):
            for copy in new:
                copy.start()
            copies.extend(new)
            return new

        theirs = pl.ds(pl.multiple_of((1 - core) * HALF + j * CHUNK, CHUNK), CHUNK)
        new = [remote(pg.at[rnd, theirs, :], crb.at[rnd, j], co_s.at[rnd, j], co_r.at[rnd, j], partner)]
        if j == 0:
            new.append(remote(wacc.at[rnd], wcb.at[rnd], co_s.at[rnd, PAIRS], co_r.at[rnd, PAIRS], partner))
        new = go(new)
        yield
        for copy in new:
            copy.wait_recv()
        mine = pl.ds(pl.multiple_of(core * HALF + j * CHUNK, CHUNK), CHUNK)
        hs[rnd, j, :, 0:piece, :] = (pg[rnd, mine, :] + crb[rnd, j]).reshape(X * Y, piece, WIN)
        if j == 0:
            hs[rnd, j, :, piece:, :] = jnp.broadcast_to((wacc[rnd] + wcb[rnd])[None], (X * Y, 8, WIN))
        new = []
        for d in range(1, X * Y):
            device, pq = xy_peer(d)
            new.append(remote(hs.at[rnd, j, pq, n, :], rxb.at[rnd, j, q, n, :], xy_s.at[rnd, j, d], xy_r.at[rnd, j, d], device))
        new = go(new)
        rxb[rnd, j, q, 0:rows, :] = hs[rnd, j, q, 0:rows, :]
        yield
        for copy in new:
            copy.wait_recv()
        total = rxb[rnd, j, 0, 0:rows, :]
        for i in range(1, X * Y):
            total = total + rxb[rnd, j, i, 0:rows, :]
        zbuf[rnd, j, z, 0:rows, :] = total
        here = zbuf.at[rnd, j, z, n, :]
        new = go([remote(here, here, z_s.at[rnd, j, d], z_r.at[rnd, j, d], z_peer(d)) for d in range(1, nz)])
        yield
        for copy in new:
            copy.wait_recv()
        total = zbuf[rnd, j, 0, 0:rows, :]
        for i in range(1, nz):
            total = total + zbuf[rnd, j, i, 0:rows, :]
        if j == 0:
            wcb[rnd] = jnp.broadcast_to(jnp.sum(total[piece:], axis=(0, 1), keepdims=True), (8, WIN))
        scale = PROBE_RELAX * WIN * WIN / wcb[rnd, 0:1, :]
        base = core * HALF + j * CHUNK
        place = pl.ds(pl.multiple_of(base + q * piece, piece), piece)
        pn[rnd, place, :] = probe_now[place, :] + scale * total[:piece]
        here = pn.at[rnd, place, :]
        new = go([remote(here, here, ag_s.at[rnd, j, d], ag_r.at[rnd, j, d], xy_peer(d)[0]) for d in range(1, X * Y)])
        yield
        forwards = []
        for dx in (0, 1, 3, 2) if X == 4 else range(X):
            for d in range(dx * Y, (dx + 1) * Y):
                if d:
                    new[d - 1].wait_recv()
            group = ((x + X - dx) % X) * Y * piece
            source = pn.at[rnd, pl.ds(pl.multiple_of(base + group, Y * piece), Y * piece), :]
            forwards += go([remote(source, source, fw_s.at[rnd, j, dx], fw_r.at[rnd, j, dx], partner)])
        yield
        for copy in forwards:
            copy.wait_recv()
        sent.append([(copy, True, True) for copy in copies])
        yield

    for rnd in range(ROUNDS):
        last = rnd == ROUNDS - 1
        probe_now = probe if rnd == 0 else pn.at[rnd - 1]
        if rnd == 0:
            windows(rnd)
            forward(probe_now, 0)
        forward(probe_now, 1)
        backward(rnd, probe_now, 0, 0, SCANS)
        chunk0, chunk1 = all_reduce(rnd, probe_now, 0), all_reduce(rnd, probe_now, 1)
        next(chunk0)
        backward(rnd, probe_now, 1, 0, SCANS - 1)
        next(chunk0)
        backward(rnd, probe_now, 1, SCANS - 1, SCANS)
        next(chunk1)
        lrp[rnd, 0], _ = pack(gq[rnd, 0, 0], gq[rnd, 0, 1], low2)
        _, lrp[rnd, 1] = pack(gq[rnd, 1, 0], gq[rnd, 1, 1], low2)
        lr = [
            (remote(lrp.at[rnd, 1], lrb.at[rnd, 0], lr_s.at[rnd, 0], lr_r.at[rnd, 0], (ty, right)), has_right, has_left),
            (remote(lrp.at[rnd, 0], lrb.at[rnd, 1], lr_s.at[rnd, 1], lr_r.at[rnd, 1], (ty, left)), has_left, has_right),
        ]
        start(lr)
        next(chunk1)
        wait_recv(lr)
        for comp in range(2):
            own = jnp.where(low2, pltpu.roll(gq[rnd, 0, comp], 64, 1), pltpu.roll(gq[rnd, 1, comp], 64, 1))
            a, b = lrb[rnd, 0], lrb[rnd, 1]
            if comp == 0:
                other = jnp.where(low2, a, pltpu.roll(b, 64, 1))
            else:
                other = jnp.where(low2, pltpu.roll(a, 64, 1), b)
            mb[rnd, comp] = own + other
        n = 64 if last else 128
        ud = [
            (remote(mb.at[rnd, :, pl.ds(256 - n, n), :], udb.at[rnd, 0, :, pl.ds(0, n), :], ud_s.at[rnd, 0], ud_r.at[rnd, 0], (down, tx)), has_down, has_up),
            (remote(mb.at[rnd, :, pl.ds(0, n), :], udb.at[rnd, 1, :, pl.ds(0, n), :], ud_s.at[rnd, 1], ud_r.at[rnd, 1], (up, tx)), has_up, has_down),
        ]
        start(ud)
        next(chunk0)
        next(chunk1)
        next(chunk0)
        next(chunk1)
        next(chunk0)
        next(chunk1)
        wait_recv(ud)
        if last:
            for comp in range(2):
                add = jnp.concatenate([udb[rnd, 0, comp, 0:64, :], udb[rnd, 1, comp, 0:64, :]], axis=0)
                obj_out[comp] = objm[rnd, comp, 64:192, :] + OBJECT_STEP * (mb[rnd, comp, 64:192, :] + add)
            sent += [lr, ud]
        else:
            row = lax.broadcasted_iota(jnp.int32, (WIN, WIN), 0)
            there = ((row >= 64) | has_up, (row < 64) | has_down)
            for comp in range(2):
                for half in range(2):
                    rows = slice(half * WIN, (half + 1) * WIN)
                    add = mb[rnd, comp, rows, :] + udb[rnd, half, comp]
                    objm[rnd + 1, comp, rows, :] = objm[rnd, comp, rows, :] + jnp.where(there[half], OBJECT_STEP * add, 0.0)
            pk[rnd + 1, 0], pk[rnd + 1, 1] = pack(objm[rnd + 1, 0], objm[rnd + 1, 1], low2)
            side = [
                (remote(pk.at[rnd + 1, 1], hlr.at[rnd + 1, 0], halo_s.at[8 + 2 * rnd], halo_r.at[8 + 2 * rnd], (ty, right)), has_right, has_left),
                (remote(pk.at[rnd + 1, 0], hlr.at[rnd + 1, 1], halo_s.at[9 + 2 * rnd], halo_r.at[9 + 2 * rnd], (ty, left)), has_left, has_right),
            ]
            start(side)
            sent += [lr, ud, side]
        next(chunk0)
        if not last:
            wait_recv(side)
            windows(rnd + 1)
            forward(pn.at[rnd], 0)
        next(chunk1)
    for copies in sent:
        wait_send(copies)
    probe_out[...] = pn[ROUNDS - 1]


def per_device(object_field, probe, intensities, positions):
    nq, nz = X * Y, ZH * ZL
    slot = CHUNK // nq + 8
    vmem = lambda *shape, dtype=F32: pltpu.VMEM(shape, dtype)
    dma = lambda *shape: pltpu.SemaphoreType.DMA(shape)
    r = ROUNDS
    full = pl.BlockSpec(memory_space=pltpu.VMEM)
    hbm = pl.BlockSpec(memory_space=pltpu.MemorySpace.HBM)
    obj, new_probe = pl.pallas_call(
        kernel,
        out_shape=(
            jax.ShapeDtypeStruct((2, WIN, WIN), F32),
            jax.ShapeDtypeStruct((2 * HALF, WIN), F32),
        ),
        in_specs=[hbm, hbm, hbm, pl.BlockSpec(memory_space=pltpu.SMEM), hbm],
        out_specs=(full, full),
        scratch_shapes=[
            vmem(2 * HALF, WIN),
            vmem(SCANS, WIN, WIN),
            vmem(4, 256, 256, dtype=BF16),
            vmem(r, 2, 256, 128),
            vmem(r, 2, 256, 128),
            vmem(r, 2, 256, 128),
            vmem(2, 2, 256, 128),
            vmem(2, 2, 384, 128),
            vmem(r, 2, 2, 256, 128),
            vmem(r, 2, 256, 128),
            vmem(r, 2, 256, 128),
            vmem(r, 2, 256, 128),
            vmem(r, 2, 2, 128, 128),
            vmem(SCANS, PAIRS, 256, 256),
            vmem(SCANS, 128, 128),
            vmem(SCANS, 2, 128, 128),
            vmem(SCANS, 2, 128, 128),
            vmem(r, 2 * HALF, 128),
            vmem(r, 8, 128),
            vmem(r, PAIRS, CHUNK, 128),
            vmem(r, 8, 128),
            vmem(r, PAIRS, nq, slot, 128),
            vmem(r, PAIRS, nq, slot, 128),
            vmem(r, PAIRS, nz, slot, 128),
            vmem(r, 2 * HALF, 128),
            dma(4),
            dma(8 + 2 * r), dma(8 + 2 * r),
            dma(r, 2), dma(r, 2),
            dma(r, 2), dma(r, 2),
            dma(r, PAIRS + 1), dma(r, PAIRS + 1),
            dma(r, PAIRS, nq), dma(r, PAIRS, nq),
            dma(r, PAIRS, nz), dma(r, PAIRS, nz),
            dma(r, PAIRS, nq), dma(r, PAIRS, nq),
            dma(r, PAIRS, X), dma(r, PAIRS, X),
        ],
        compiler_params=pltpu.CompilerParams(
            collective_id=0, has_side_effects=True, vmem_limit_bytes=66_000_000
        ),
    )(
        object_field,
        probe.reshape(2 * HALF, WIN),
        intensities.reshape(SCANS, WIN, WIN),
        positions.reshape(SCANS, 2),
        jnp.asarray(dft_tables()),
    )
    return obj, new_probe.reshape(2, MODES, WIN, WIN)


def solution(mesh):
    placed = (P(None, "ty", "tx"), P(), P("ty", "tx", None, None, None), P("ty", "tx", None, None))
    return jax.shard_map(
        per_device,
        mesh=mesh,
        in_specs=placed,
        out_specs=(P(None, "ty", "tx"), P()),
        check_vma=False,
    )
```

```python
import jax
import jax.numpy as jnp
import ml_dtypes
import numpy as np
from jax import lax
from jax.experimental import pallas as pl
from jax.experimental.pallas import tpu as pltpu
from jax.sharding import PartitionSpec as P

ROUNDS = 2
OBJECT_STEP = 0.1
PROBE_RELAX = 0.5
WIN = 128
MODES = 4
SCANS = 3
PAIRS = MODES // 2
X, Y, ZH, ZL = 4, 4, 2, 4
HALF = MODES * WIN
CHUNK = HALF // PAIRS
MESH = pl.DeviceIdType.MESH
MIDDLE = ""
FIRST = "10o101o01o010o"
LAST = "10o101o01o0101"
F32, BF16 = jnp.float32, jnp.bfloat16


def dft_tables():
    line = np.arange(WIN)
    angle = (line[:, None] * line[None, :] % WIN) * (2.0 * np.pi / WIN)
    c, s = np.cos(angle) * WIN**-0.5, np.sin(angle) * WIN**-0.5
    a = np.block([[c, -s], [s, c]])
    parts = []
    for m in (a, a.T):
        hi = m.astype(ml_dtypes.bfloat16)
        lo = (m - hi.astype(np.float64)).astype(ml_dtypes.bfloat16)
        parts += [hi, lo]
    return np.stack(parts)


def split(x):
    hi = x.astype(BF16)
    return hi, (x - hi.astype(F32)).astype(BF16)


def mm(a, b):
    return jnp.dot(a, b, preferred_element_type=F32)


def left_mm(tab, i, x):
    hi, lo = split(x)
    return mm(tab[i], hi) + mm(tab[i], lo) + mm(tab[i + 1], hi)


def right_mm(x, tab, i):
    hi, lo = split(x)
    return mm(hi, tab[i]) + mm(lo, tab[i]) + mm(hi, tab[i + 1])


def regroup(t):
    top = jnp.concatenate([t[:WIN, :WIN], t[WIN:, :WIN]], axis=1)
    bottom = jnp.concatenate([t[:WIN, WIN:], t[WIN:, WIN:]], axis=1)
    return jnp.concatenate([top, bottom], axis=0)


def kernel(
    obj_hbm, probe_hbm, inten_hbm, pos, tab_hbm, obj_out, probe_out,
    probe, inten, tab, objm, hlr, pk, ext, zp, gq, lrp, lrb, mb, udb, uf, pw, win, gs, pg, wacc,
    crb, wcb, hs, rxb, zbuf, pn,
    in_s, halo_s, halo_r, lr_s, lr_r, ud_s, ud_r, co_s, co_r, xy_s, xy_r, z_s, z_r, ag_s, ag_r, fw_s, fw_r,
):
    ty, tx = lax.axis_index("ty"), lax.axis_index("tx")
    nty, ntx = ZH * X, ZL * Y * 2
    zh, x = ty // X, ty % X
    zl, y, core = tx // (2 * Y), (tx // 2) % Y, tx % 2
    z = zh * ZL + zl
    q = x * Y + y
    piece = CHUNK // (X * Y)
    nz = ZH * ZL

    has_up, has_down = ty > 0, ty < nty - 1
    has_left, has_right = tx > 0, tx < ntx - 1
    up, down = (ty + nty - 1) % nty, (ty + 1) % nty
    left, right = (tx + ntx - 1) % ntx, (tx + 1) % ntx
    partner = (ty, tx + 1 - 2 * core)

    def xy_peer(d):
        px, py = (x + d // Y) % X, (y + d % Y) % Y
        return (zh * X + px, zl * 2 * Y + py * 2 + core), px * Y + py

    def z_peer(d):
        pz = (z + d) % nz
        return ((pz // ZL) * X + x, (pz % ZL) * 2 * Y + y * 2 + core)

    ring = lambda d, n: min(d, n - d)
    far_xy = sorted(range(X * Y - 1), key=lambda i: -ring((i + 1) // Y, X) - ring((i + 1) % Y, Y))
    far_z = sorted(range(nz - 1), key=lambda i: -ring(i + 1, nz))

    def remote(src, dst, ssem, rsem, device):
        return pltpu.make_async_remote_copy(
            src_ref=src, dst_ref=dst, send_sem=ssem, recv_sem=rsem, device_id=device, device_id_type=MESH
        )

    loads = [
        pltpu.make_async_copy(obj_hbm, objm.at[0, :, pl.ds(64, WIN), :], in_s.at[0]),
        pltpu.make_async_copy(probe_hbm, probe, in_s.at[1]),
        pltpu.make_async_copy(tab_hbm, tab, in_s.at[2]),
        pltpu.make_async_copy(inten_hbm, inten, in_s.at[3]),
    ]
    for copy in loads:
        copy.start()
    peers = [partner, (ty, left), (ty, right), (up, tx), (down, tx), (up, left), (up, right), (down, left), (down, right)]
    peers += [xy_peer(d)[0] for d in range(1, X * Y)] + [z_peer(d) for d in range(1, nz)]
    barrier = pltpu.get_barrier_semaphore()
    for peer in peers:
        pl.semaphore_signal(barrier, inc=1, device_id=peer, device_id_type=MESH)

    low = lax.broadcasted_iota(jnp.int32, (WIN, WIN), 1) < 64
    lane = lax.broadcasted_iota(jnp.int32, (WIN, WIN), 1)
    low2 = lax.broadcasted_iota(jnp.int32, (2 * WIN, WIN), 1) < 64
    zp[...] = jnp.zeros_like(zp)
    loads[0].wait()

    def pack(re, im, low):
        return jnp.where(low, re, pltpu.roll(im, 64, 1)), jnp.where(low, pltpu.roll(re, 64, 1), im)

    pk[0, 0, 64:192, :], pk[0, 1, 64:192, :] = pack(objm[0, 0, 64:192, :], objm[0, 1, 64:192, :], low)

    @pl.when(jnp.logical_not(has_left))
    def _():
        hlr[:, 0] = jnp.zeros_like(hlr.at[:, 0])
        lrb[:, 0] = jnp.zeros_like(lrb.at[:, 0])

    @pl.when(jnp.logical_not(has_right))
    def _():
        hlr[:, 1] = jnp.zeros_like(hlr.at[:, 1])
        lrb[:, 1] = jnp.zeros_like(lrb.at[:, 1])

    @pl.when(jnp.logical_not(has_up))
    def _():
        hlr[0, :, 0:64, :] = jnp.zeros((2, 64, WIN), F32)
        objm[0, :, 0:64, :] = jnp.zeros((2, 64, WIN), F32)
        udb[:, 0] = jnp.zeros_like(udb.at[:, 0])

    @pl.when(jnp.logical_not(has_down))
    def _():
        hlr[0, :, 192:256, :] = jnp.zeros((2, 64, WIN), F32)
        objm[0, :, 192:256, :] = jnp.zeros((2, 64, WIN), F32)
        udb[:, 1] = jnp.zeros_like(udb.at[:, 1])

    pl.semaphore_wait(barrier, len(peers))

    def start(copies):
        for copy, to, _ in copies:
            @pl.when(to)
            def _():
                copy.start()

    def wait_recv(copies):
        for copy, _, came in copies:
            @pl.when(came)
            def _():
                copy.wait_recv()

    def wait_send(copies):
        for copy, to, _ in copies:
            @pl.when(to)
            def _():
                copy.wait_send()

    top, bottom, mid = pl.ds(64, 64), pl.ds(128, 64), pl.ds(64, 128)
    above, below = pl.ds(0, 64), pl.ds(192, 64)
    halo = [
        (objm.at[0, :, bottom, :], objm.at[0, :, above, :], (down, tx), has_down, has_up),
        (objm.at[0, :, top, :], objm.at[0, :, below, :], (up, tx), has_up, has_down),
        (pk.at[0, 1, mid, :], hlr.at[0, 0, mid, :], (ty, right), has_right, has_left),
        (pk.at[0, 0, mid, :], hlr.at[0, 1, mid, :], (ty, left), has_left, has_right),
        (pk.at[0, 1, bottom, :], hlr.at[0, 0, above, :], (down, right), has_down & has_right, has_up & has_left),
        (pk.at[0, 0, bottom, :], hlr.at[0, 1, above, :], (down, left), has_down & has_left, has_up & has_right),
        (pk.at[0, 1, top, :], hlr.at[0, 0, below, :], (up, right), has_up & has_right, has_down & has_left),
        (pk.at[0, 0, top, :], hlr.at[0, 1, below, :], (up, left), has_up & has_left, has_down & has_right),
    ]
    halo = [(remote(s, d, halo_s.at[i], halo_r.at[i], p), to, came) for i, (s, d, p, to, came) in enumerate(halo)]
    start(halo)
    for copy in loads[1:]:
        copy.wait()
    sent = [halo]
    wait_recv(halo)

    def windows(rnd):
        m_re, m_im = pltpu.roll(objm[rnd, 0], 64, 1), pltpu.roll(objm[rnd, 1], 64, 1)
        fl, fr = hlr[rnd, 0], hlr[rnd, 1]
        ext[0, 0] = jnp.where(low2, fl, m_re)
        ext[0, 1] = jnp.where(low2, pltpu.roll(fl, 64, 1), m_im)
        ext[1, 0] = jnp.where(low2, m_re, pltpu.roll(fr, 64, 1))
        ext[1, 1] = jnp.where(low2, m_im, fr)
        wacc[rnd] = jnp.zeros_like(wacc.at[rnd])
        gq[rnd] = jnp.zeros_like(gq.at[rnd])
        pg[rnd] = jnp.zeros_like(pg.at[rnd])

        def cut(s, carry):
            r, c = pos[0, s], pos[1, s]
            back = (WIN - c) & (WIN - 1)
            first = lane + c < WIN
            w = wacc[rnd]
            for comp in range(2):
                x0 = pltpu.roll(ext[0, comp, pl.ds(r, WIN), :], back, 1)
                x1 = pltpu.roll(ext[1, comp, pl.ds(r, WIN), :], back, 1)
                o = jnp.where(first, x0, x1)
                win[s, comp] = o
                w = w + jnp.sum((o * o).reshape(WIN // 8, 8, WIN), axis=0)
            wacc[rnd] = w
            return carry

        lax.fori_loop(0, SCANS, cut, 0, unroll=True)

    def modes_of(ref, j):
        return [
            (ref[k * WIN : (k + 1) * WIN, :], ref[HALF + k * WIN : HALF + (k + 1) * WIN, :])
            for k in range(2 * j, 2 * j + 2)
        ]

    def forward(probe_now, j):
        def step(s, carry):
            w_re, w_im = win[s, 0], win[s, 1]
            (a_re, a_im), (b_re, b_im) = modes_of(probe_now, j)
            wave_re = jnp.concatenate([a_re * w_re - a_im * w_im, b_re * w_re - b_im * w_im], axis=1)
            wave_im = jnp.concatenate([a_re * w_im + a_im * w_re, b_re * w_im + b_im * w_re], axis=1)
            t = left_mm(tab, 2, jnp.concatenate([wave_re, wave_im], axis=0))
            u = right_mm(regroup(t), tab, 0)
            uf[s, j] = u
            u2 = u * u
            p = (u2[:WIN, :WIN] + u2[:WIN, WIN:]) + (u2[WIN:, :WIN] + u2[WIN:, WIN:])
            if j == 0:
                pw[s] = p
            else:
                p = pw[s] + p
                pw[s] = jnp.sqrt(inten[s]) / jnp.sqrt(jnp.maximum(p, 1.0)) - 1.0
            return carry

        lax.fori_loop(0, SCANS, step, 0, unroll=True)

    def backward(rnd, probe_now, j, lo, hi):
        def step(s, carry):
            f = jnp.concatenate([pw[s], pw[s]], axis=1)
            b = right_mm(uf[s, j] * jnp.concatenate([f, f], axis=0), tab, 2)
            t = left_mm(tab, 0, regroup(b))
            w_re, w_im = win[s, 0], win[s, 1]
            g_re, g_im = (0.0, 0.0) if j == 0 else (gs[s, 0], gs[s, 1])
            for i, (p_re, p_im) in enumerate(modes_of(probe_now, j)):
                k = 2 * j + i
                b_re, b_im = t[:WIN, i * WIN : (i + 1) * WIN], t[WIN:, i * WIN : (i + 1) * WIN]
                g_re = g_re + p_re * b_re + p_im * b_im
                g_im = g_im + p_re * b_im - p_im * b_re
                pg[rnd, k * WIN : (k + 1) * WIN, :] += w_re * b_re + w_im * b_im
                pg[rnd, HALF + k * WIN : HALF + (k + 1) * WIN, :] += w_re * b_im - w_im * b_re
            if j < PAIRS - 1:
                gs[s, 0], gs[s, 1] = g_re, g_im
            else:
                r, c = pos[0, s], pos[1, s]
                turn = c & (WIN - 1)
                inside = lane >= c
                for comp, g in enumerate((g_re, g_im)):
                    g = pltpu.roll(g, turn, 1)
                    zp[0, comp, WIN : 2 * WIN, :] = jnp.where(inside, g, 0.0)
                    zp[1, comp, WIN : 2 * WIN, :] = jnp.where(inside, 0.0, g)
                for half in range(2):
                    for comp in range(2):
                        gq[rnd, half, comp] += zp[half, comp, pl.ds(WIN - r, 2 * WIN), :]
            return carry

        lax.fori_loop(lo, hi, step, 0, unroll=True)

    def all_reduce(rnd, probe_now, j):
        rows = piece + (8 if j == 0 else 0)
        n = pl.ds(0, rows)
        copies = []

        def go(new, order=None):
            for i in order or range(len(new)):
                new[i].start()
            copies.extend(new)
            return new

        theirs = pl.ds(pl.multiple_of((1 - core) * HALF + j * CHUNK, CHUNK), CHUNK)
        new = [remote(pg.at[rnd, theirs, :], crb.at[rnd, j], co_s.at[rnd, j], co_r.at[rnd, j], partner)]
        if j == 0:
            new.append(remote(wacc.at[rnd], wcb.at[rnd], co_s.at[rnd, PAIRS], co_r.at[rnd, PAIRS], partner))
        new = go(new)
        yield
        for copy in new:
            copy.wait_recv()
        mine = pl.ds(pl.multiple_of(core * HALF + j * CHUNK, CHUNK), CHUNK)
        hs[rnd, j, :, 0:piece, :] = (pg[rnd, mine, :] + crb[rnd, j]).reshape(X * Y, piece, WIN)
        if j == 0:
            hs[rnd, j, :, piece:, :] = jnp.broadcast_to((wacc[rnd] + wcb[rnd])[None], (X * Y, 8, WIN))
        new = []
        for d in range(1, X * Y):
            device, pq = xy_peer(d)
            new.append(remote(hs.at[rnd, j, pq, n, :], rxb.at[rnd, j, q, n, :], xy_s.at[rnd, j, d], xy_r.at[rnd, j, d], device))
        new = go(new, far_xy)
        rxb[rnd, j, q, 0:rows, :] = hs[rnd, j, q, 0:rows, :]
        yield
        for copy in new:
            copy.wait_recv()
        total = rxb[rnd, j, 0, 0:rows, :]
        for i in range(1, X * Y):
            total = total + rxb[rnd, j, i, 0:rows, :]
        zbuf[rnd, j, z, 0:rows, :] = total
        here = zbuf.at[rnd, j, z, n, :]
        new = go([remote(here, here, z_s.at[rnd, j, d], z_r.at[rnd, j, d], z_peer(d)) for d in range(1, nz)], far_z)
        yield
        for copy in new:
            copy.wait_recv()
        total = zbuf[rnd, j, 0, 0:rows, :]
        for i in range(1, nz):
            total = total + zbuf[rnd, j, i, 0:rows, :]
        if j == 0:
            wcb[rnd] = jnp.broadcast_to(jnp.sum(total[piece:], axis=(0, 1), keepdims=True), (8, WIN))
        scale = PROBE_RELAX * WIN * WIN / wcb[rnd, 0:1, :]
        base = core * HALF + j * CHUNK
        place = pl.ds(pl.multiple_of(base + q * piece, piece), piece)
        pn[rnd, place, :] = probe_now[place, :] + scale * total[:piece]
        here = pn.at[rnd, place, :]
        new = go([remote(here, here, ag_s.at[rnd, j, d], ag_r.at[rnd, j, d], xy_peer(d)[0]) for d in range(1, X * Y)], far_xy)
        yield
        forwards = []
        for dx in (0, 1, 3, 2) if X == 4 else range(X):
            for d in range(dx * Y, (dx + 1) * Y):
                if d:
                    new[d - 1].wait_recv()
            group = ((x + X - dx) % X) * Y * piece
            source = pn.at[rnd, pl.ds(pl.multiple_of(base + group, Y * piece), Y * piece), :]
            forwards += go([remote(source, source, fw_s.at[rnd, j, dx], fw_r.at[rnd, j, dx], partner)])
        yield
        for copy in forwards:
            copy.wait_recv()
        sent.append([(copy, True, True) for copy in copies])
        yield

    def object_exchange(rnd, last):
        lrp[rnd, 0], _ = pack(gq[rnd, 0, 0], gq[rnd, 0, 1], low2)
        _, lrp[rnd, 1] = pack(gq[rnd, 1, 0], gq[rnd, 1, 1], low2)
        lr = [
            (remote(lrp.at[rnd, 1], lrb.at[rnd, 0], lr_s.at[rnd, 0], lr_r.at[rnd, 0], (ty, right)), has_right, has_left),
            (remote(lrp.at[rnd, 0], lrb.at[rnd, 1], lr_s.at[rnd, 1], lr_r.at[rnd, 1], (ty, left)), has_left, has_right),
        ]
        start(lr)
        yield
        wait_recv(lr)
        a, b = lrb[rnd, 0], lrb[rnd, 1]
        others = (jnp.where(low2, a, pltpu.roll(b, 64, 1)), jnp.where(low2, pltpu.roll(a, 64, 1), b))
        for comp, other in enumerate(others):
            own = jnp.where(low2, pltpu.roll(gq[rnd, 0, comp], 64, 1), pltpu.roll(gq[rnd, 1, comp], 64, 1))
            mb[rnd, comp] = own + other
        n = 64 if last else 128
        ud = [
            (remote(mb.at[rnd, :, pl.ds(256 - n, n), :], udb.at[rnd, 0, :, pl.ds(0, n), :], ud_s.at[rnd, 0], ud_r.at[rnd, 0], (down, tx)), has_down, has_up),
            (remote(mb.at[rnd, :, pl.ds(0, n), :], udb.at[rnd, 1, :, pl.ds(0, n), :], ud_s.at[rnd, 1], ud_r.at[rnd, 1], (up, tx)), has_up, has_down),
        ]
        start(ud)
        sent.extend([lr, ud])
        yield
        wait_recv(ud)
        if last:
            for comp in range(2):
                add = jnp.concatenate([udb[rnd, 0, comp, 0:64, :], udb[rnd, 1, comp, 0:64, :]], axis=0)
                obj_out[comp] = objm[rnd, comp, 64:192, :] + OBJECT_STEP * (mb[rnd, comp, 64:192, :] + add)
            yield
            return
        row = lax.broadcasted_iota(jnp.int32, (WIN, WIN), 0)
        there = ((row >= 64) | has_up, (row < 64) | has_down)
        for comp in range(2):
            for half in range(2):
                rows = slice(half * WIN, (half + 1) * WIN)
                add = mb[rnd, comp, rows, :] + udb[rnd, half, comp]
                objm[rnd + 1, comp, rows, :] = objm[rnd, comp, rows, :] + jnp.where(there[half], OBJECT_STEP * add, 0.0)
        pk[rnd + 1, 0], pk[rnd + 1, 1] = pack(objm[rnd + 1, 0], objm[rnd + 1, 1], low2)
        side = [
            (remote(pk.at[rnd + 1, 1], hlr.at[rnd + 1, 0], halo_s.at[8 + 2 * rnd], halo_r.at[8 + 2 * rnd], (ty, right)), has_right, has_left),
            (remote(pk.at[rnd + 1, 0], hlr.at[rnd + 1, 1], halo_s.at[9 + 2 * rnd], halo_r.at[9 + 2 * rnd], (ty, left)), has_left, has_right),
        ]
        start(side)
        sent.append(side)
        yield
        wait_recv(side)
        yield

    for rnd in range(ROUNDS):
        last = rnd == ROUNDS - 1
        probe_now = probe if rnd == 0 else pn.at[rnd - 1]
        if rnd == 0:
            windows(rnd)
            forward(probe_now, 0)
        forward(probe_now, 1)
        steps = {"0": all_reduce(rnd, probe_now, 0), "1": all_reduce(rnd, probe_now, 1), "o": object_exchange(rnd, last)}

        def do(order):
            for name in order:
                next(steps[name])

        backward(rnd, probe_now, 0, 0, SCANS)
        do("0")
        backward(rnd, probe_now, 1, 0, SCANS - 1)
        do(MIDDLE)
        backward(rnd, probe_now, 1, SCANS - 1, SCANS)
        if last:
            do(LAST)
        else:
            do(FIRST)
            windows(rnd + 1)
            forward(pn.at[rnd], 0)
            do("1")
    for copies in sent:
        wait_send(copies)
    probe_out[...] = pn[ROUNDS - 1]


def per_device(object_field, probe, intensities, positions):
    nq, nz = X * Y, ZH * ZL
    slot = CHUNK // nq + 8
    vmem = lambda *shape, dtype=F32: pltpu.VMEM(shape, dtype)
    dma = lambda *shape: pltpu.SemaphoreType.DMA(shape)
    r = ROUNDS
    full = pl.BlockSpec(memory_space=pltpu.VMEM)
    hbm = pl.BlockSpec(memory_space=pltpu.MemorySpace.HBM)
    obj, new_probe = pl.pallas_call(
        kernel,
        out_shape=(
            jax.ShapeDtypeStruct((2, WIN, WIN), F32),
            jax.ShapeDtypeStruct((2 * HALF, WIN), F32),
        ),
        in_specs=[hbm, hbm, hbm, pl.BlockSpec(memory_space=pltpu.SMEM), hbm],
        out_specs=(full, full),
        scratch_shapes=[
            vmem(2 * HALF, WIN),
            vmem(SCANS, WIN, WIN),
            vmem(4, 256, 256, dtype=BF16),
            vmem(r, 2, 256, 128),
            vmem(r, 2, 256, 128),
            vmem(r, 2, 256, 128),
            vmem(2, 2, 256, 128),
            vmem(2, 2, 384, 128),
            vmem(r, 2, 2, 256, 128),
            vmem(r, 2, 256, 128),
            vmem(r, 2, 256, 128),
            vmem(r, 2, 256, 128),
            vmem(r, 2, 2, 128, 128),
            vmem(SCANS, PAIRS, 256, 256),
            vmem(SCANS, 128, 128),
            vmem(SCANS, 2, 128, 128),
            vmem(SCANS, 2, 128, 128),
            vmem(r, 2 * HALF, 128),
            vmem(r, 8, 128),
            vmem(r, PAIRS, CHUNK, 128),
            vmem(r, 8, 128),
            vmem(r, PAIRS, nq, slot, 128),
            vmem(r, PAIRS, nq, slot, 128),
            vmem(r, PAIRS, nz, slot, 128),
            vmem(r, 2 * HALF, 128),
            dma(4),
            dma(8 + 2 * r), dma(8 + 2 * r),
            dma(r, 2), dma(r, 2),
            dma(r, 2), dma(r, 2),
            dma(r, PAIRS + 1), dma(r, PAIRS + 1),
            dma(r, PAIRS, nq), dma(r, PAIRS, nq),
            dma(r, PAIRS, nz), dma(r, PAIRS, nz),
            dma(r, PAIRS, nq), dma(r, PAIRS, nq),
            dma(r, PAIRS, X), dma(r, PAIRS, X),
        ],
        compiler_params=pltpu.CompilerParams(
            collective_id=0, has_side_effects=True, vmem_limit_bytes=66_000_000
        ),
    )(
        object_field,
        probe.reshape(2 * HALF, WIN),
        intensities.reshape(SCANS, WIN, WIN),
        positions.reshape(SCANS, 2).T,
        jnp.asarray(dft_tables()),
    )
    return obj, new_probe.reshape(2, MODES, WIN, WIN)


def solution(mesh):
    placed = (P(None, "ty", "tx"), P(), P("ty", "tx", None, None, None), P("ty", "tx", None, None))
    return jax.shard_map(
        per_device,
        mesh=mesh,
        in_specs=placed,
        out_specs=(P(None, "ty", "tx"), P()),
        check_vma=False,
    )
```

```python
import jax
import jax.numpy as jnp
import ml_dtypes
import numpy as np
from jax import lax
from jax.experimental import pallas as pl
from jax.experimental.pallas import tpu as pltpu
from jax.sharding import PartitionSpec as P

ROUNDS = 2
OBJECT_STEP = 0.1
PROBE_RELAX = 0.5
WIN = 128
MODES = 4
SCANS = 3
PAIRS = MODES // 2
X, Y, ZH, ZL = 4, 4, 2, 4
HALF = MODES * WIN
CHUNK = HALF // PAIRS
MESH = pl.DeviceIdType.MESH
MIDDLE = "0"
FIRST = "1o101o010o10o"
LAST = "1o101o01o0101"
F32, BF16 = jnp.float32, jnp.bfloat16


def dft_tables():
    line = np.arange(WIN)
    angle = (line[:, None] * line[None, :] % WIN) * (2.0 * np.pi / WIN)
    c, s = np.cos(angle) * WIN**-0.5, np.sin(angle) * WIN**-0.5
    a = np.block([[c, -s], [s, c]])
    parts = []
    for m in (a, a.T):
        hi = m.astype(ml_dtypes.bfloat16)
        lo = (m - hi.astype(np.float64)).astype(ml_dtypes.bfloat16)
        parts += [hi, lo]
    return np.stack(parts)


def split(x):
    hi = x.astype(BF16)
    return hi, (x - hi.astype(F32)).astype(BF16)


def mm(a, b):
    return jnp.dot(a, b, preferred_element_type=F32)


def left_mm(tab, i, x):
    hi, lo = split(x)
    return mm(tab[i], hi) + mm(tab[i], lo) + mm(tab[i + 1], hi)


def right_mm(x, tab, i):
    hi, lo = split(x)
    return mm(hi, tab[i]) + mm(lo, tab[i]) + mm(hi, tab[i + 1])


def regroup(t):
    top = jnp.concatenate([t[:WIN, :WIN], t[WIN:, :WIN]], axis=1)
    bottom = jnp.concatenate([t[:WIN, WIN:], t[WIN:, WIN:]], axis=1)
    return jnp.concatenate([top, bottom], axis=0)


def kernel(
    obj_hbm, probe_hbm, inten_hbm, pos, tab_hbm, obj_hbm_out, probe_hbm_out, obj_out,
    probe, inten, tab, objm, hlr, pk, ext, zp, gq, lrp, lrb, mb, udb, uf, pw, win, gs, pg, wacc,
    crb, wcb, hs, rxb, zbuf, pn,
    in_s, halo_s, halo_r, lr_s, lr_r, ud_s, ud_r, co_s, co_r, xy_s, xy_r, z_s, z_r, ag_s, ag_r, fw_s, fw_r,
):
    ty, tx = lax.axis_index("ty"), lax.axis_index("tx")
    nty, ntx = ZH * X, ZL * Y * 2
    zh, x = ty // X, ty % X
    zl, y, core = tx // (2 * Y), (tx // 2) % Y, tx % 2
    z = zh * ZL + zl
    q = x * Y + y
    piece = CHUNK // (X * Y)
    nz = ZH * ZL

    has_up, has_down = ty > 0, ty < nty - 1
    has_left, has_right = tx > 0, tx < ntx - 1
    up, down = (ty + nty - 1) % nty, (ty + 1) % nty
    left, right = (tx + ntx - 1) % ntx, (tx + 1) % ntx
    partner = (ty, tx + 1 - 2 * core)

    def xy_peer(d):
        px, py = (x + d // Y) % X, (y + d % Y) % Y
        return (zh * X + px, zl * 2 * Y + py * 2 + core), px * Y + py

    def z_peer(d):
        pz = (z + d) % nz
        return ((pz // ZL) * X + x, (pz % ZL) * 2 * Y + y * 2 + core)

    ring = lambda d, n: min(d, n - d)
    far_xy = sorted(range(X * Y - 1), key=lambda i: -ring((i + 1) // Y, X) - ring((i + 1) % Y, Y))
    far_z = sorted(range(nz - 1), key=lambda i: -ring(i + 1, nz))

    def remote(src, dst, ssem, rsem, device):
        return pltpu.make_async_remote_copy(
            src_ref=src, dst_ref=dst, send_sem=ssem, recv_sem=rsem, device_id=device, device_id_type=MESH
        )

    loads = [
        pltpu.make_async_copy(obj_hbm, objm.at[0, :, pl.ds(64, WIN), :], in_s.at[0]),
        pltpu.make_async_copy(probe_hbm, probe, in_s.at[1]),
        pltpu.make_async_copy(tab_hbm, tab, in_s.at[2]),
        pltpu.make_async_copy(inten_hbm, inten, in_s.at[3]),
    ]
    for copy in loads:
        copy.start()
    peers = [partner, (ty, left), (ty, right), (up, tx), (down, tx), (up, left), (up, right), (down, left), (down, right)]
    peers += [xy_peer(d)[0] for d in range(1, X * Y)] + [z_peer(d) for d in range(1, nz)]
    barrier = pltpu.get_barrier_semaphore()
    for peer in peers:
        pl.semaphore_signal(barrier, inc=1, device_id=peer, device_id_type=MESH)

    low = lax.broadcasted_iota(jnp.int32, (WIN, WIN), 1) < 64
    lane = lax.broadcasted_iota(jnp.int32, (WIN, WIN), 1)
    low2 = lax.broadcasted_iota(jnp.int32, (2 * WIN, WIN), 1) < 64
    zp[...] = jnp.zeros_like(zp)
    loads[0].wait()

    def pack(re, im, low):
        return jnp.where(low, re, pltpu.roll(im, 64, 1)), jnp.where(low, pltpu.roll(re, 64, 1), im)

    pk[0, 0, 64:192, :], pk[0, 1, 64:192, :] = pack(objm[0, 0, 64:192, :], objm[0, 1, 64:192, :], low)

    @pl.when(jnp.logical_not(has_left))
    def _():
        hlr[:, 0] = jnp.zeros_like(hlr.at[:, 0])
        lrb[:, 0] = jnp.zeros_like(lrb.at[:, 0])

    @pl.when(jnp.logical_not(has_right))
    def _():
        hlr[:, 1] = jnp.zeros_like(hlr.at[:, 1])
        lrb[:, 1] = jnp.zeros_like(lrb.at[:, 1])

    @pl.when(jnp.logical_not(has_up))
    def _():
        hlr[0, :, 0:64, :] = jnp.zeros((2, 64, WIN), F32)
        objm[0, :, 0:64, :] = jnp.zeros((2, 64, WIN), F32)
        udb[:, 0] = jnp.zeros_like(udb.at[:, 0])

    @pl.when(jnp.logical_not(has_down))
    def _():
        hlr[0, :, 192:256, :] = jnp.zeros((2, 64, WIN), F32)
        objm[0, :, 192:256, :] = jnp.zeros((2, 64, WIN), F32)
        udb[:, 1] = jnp.zeros_like(udb.at[:, 1])

    pl.semaphore_wait(barrier, len(peers))

    def start(copies):
        for copy, to, _ in copies:
            @pl.when(to)
            def _():
                copy.start()

    def wait_recv(copies):
        for copy, _, came in copies:
            @pl.when(came)
            def _():
                copy.wait_recv()

    def wait_send(copies):
        for copy, to, _ in copies:
            @pl.when(to)
            def _():
                copy.wait_send()

    top, bottom, mid = pl.ds(64, 64), pl.ds(128, 64), pl.ds(64, 128)
    above, below = pl.ds(0, 64), pl.ds(192, 64)
    halo = [
        (objm.at[0, :, bottom, :], objm.at[0, :, above, :], (down, tx), has_down, has_up),
        (objm.at[0, :, top, :], objm.at[0, :, below, :], (up, tx), has_up, has_down),
        (pk.at[0, 1, mid, :], hlr.at[0, 0, mid, :], (ty, right), has_right, has_left),
        (pk.at[0, 0, mid, :], hlr.at[0, 1, mid, :], (ty, left), has_left, has_right),
        (pk.at[0, 1, bottom, :], hlr.at[0, 0, above, :], (down, right), has_down & has_right, has_up & has_left),
        (pk.at[0, 0, bottom, :], hlr.at[0, 1, above, :], (down, left), has_down & has_left, has_up & has_right),
        (pk.at[0, 1, top, :], hlr.at[0, 0, below, :], (up, right), has_up & has_right, has_down & has_left),
        (pk.at[0, 0, top, :], hlr.at[0, 1, below, :], (up, left), has_up & has_left, has_down & has_right),
    ]
    halo = [(remote(s, d, halo_s.at[i], halo_r.at[i], p), to, came) for i, (s, d, p, to, came) in enumerate(halo)]
    start(halo)
    for copy in loads[1:]:
        copy.wait()
    sent = [halo]
    wait_recv(halo)

    def windows(rnd):
        m_re, m_im = pltpu.roll(objm[rnd, 0], 64, 1), pltpu.roll(objm[rnd, 1], 64, 1)
        fl, fr = hlr[rnd, 0], hlr[rnd, 1]
        ext[0, 0] = jnp.where(low2, fl, m_re)
        ext[0, 1] = jnp.where(low2, pltpu.roll(fl, 64, 1), m_im)
        ext[1, 0] = jnp.where(low2, m_re, pltpu.roll(fr, 64, 1))
        ext[1, 1] = jnp.where(low2, m_im, fr)
        wacc[rnd] = jnp.zeros_like(wacc.at[rnd])
        gq[rnd] = jnp.zeros_like(gq.at[rnd])
        pg[rnd] = jnp.zeros_like(pg.at[rnd])

        def cut(s, carry):
            r, c = pos[0, s], pos[1, s]
            back = (WIN - c) & (WIN - 1)
            first = lane + c < WIN
            w = wacc[rnd]
            for comp in range(2):
                x0 = pltpu.roll(ext[0, comp, pl.ds(r, WIN), :], back, 1)
                x1 = pltpu.roll(ext[1, comp, pl.ds(r, WIN), :], back, 1)
                o = jnp.where(first, x0, x1)
                win[s, comp] = o
                w = w + jnp.sum((o * o).reshape(WIN // 8, 8, WIN), axis=0)
            wacc[rnd] = w
            return carry

        lax.fori_loop(0, SCANS, cut, 0, unroll=True)

    def modes_of(ref, j):
        return [
            (ref[k * WIN : (k + 1) * WIN, :], ref[HALF + k * WIN : HALF + (k + 1) * WIN, :])
            for k in range(2 * j, 2 * j + 2)
        ]

    def forward(probe_now, j):
        def step(s, carry):
            w_re, w_im = win[s, 0], win[s, 1]
            (a_re, a_im), (b_re, b_im) = modes_of(probe_now, j)
            wave_re = jnp.concatenate([a_re * w_re - a_im * w_im, b_re * w_re - b_im * w_im], axis=1)
            wave_im = jnp.concatenate([a_re * w_im + a_im * w_re, b_re * w_im + b_im * w_re], axis=1)
            t = left_mm(tab, 2, jnp.concatenate([wave_re, wave_im], axis=0))
            u = right_mm(regroup(t), tab, 0)
            uf[s, j] = u
            u2 = u * u
            p = (u2[:WIN, :WIN] + u2[:WIN, WIN:]) + (u2[WIN:, :WIN] + u2[WIN:, WIN:])
            if j == 0:
                pw[s] = p
            else:
                p = pw[s] + p
                pw[s] = jnp.sqrt(inten[s]) / jnp.sqrt(jnp.maximum(p, 1.0)) - 1.0
            return carry

        lax.fori_loop(0, SCANS, step, 0, unroll=True)

    def backward(rnd, probe_now, j, lo, hi):
        def step(s, carry):
            f = jnp.concatenate([pw[s], pw[s]], axis=1)
            b = right_mm(uf[s, j] * jnp.concatenate([f, f], axis=0), tab, 2)
            t = left_mm(tab, 0, regroup(b))
            w_re, w_im = win[s, 0], win[s, 1]
            g_re, g_im = (0.0, 0.0) if j == 0 else (gs[s, 0], gs[s, 1])
            for i, (p_re, p_im) in enumerate(modes_of(probe_now, j)):
                k = 2 * j + i
                b_re, b_im = t[:WIN, i * WIN : (i + 1) * WIN], t[WIN:, i * WIN : (i + 1) * WIN]
                g_re = g_re + p_re * b_re + p_im * b_im
                g_im = g_im + p_re * b_im - p_im * b_re
                pg[rnd, k * WIN : (k + 1) * WIN, :] += w_re * b_re + w_im * b_im
                pg[rnd, HALF + k * WIN : HALF + (k + 1) * WIN, :] += w_re * b_im - w_im * b_re
            gs[s, 0], gs[s, 1] = g_re, g_im
            return carry

        lax.fori_loop(lo, hi, step, 0, unroll=True)

    def place(rnd):
        def step(s, carry):
            r, c = pos[0, s], pos[1, s]
            turn = c & (WIN - 1)
            inside = lane >= c
            for comp in range(2):
                g = pltpu.roll(gs[s, comp], turn, 1)
                zp[0, comp, WIN : 2 * WIN, :] = jnp.where(inside, g, 0.0)
                zp[1, comp, WIN : 2 * WIN, :] = jnp.where(inside, 0.0, g)
            for half in range(2):
                for comp in range(2):
                    gq[rnd, half, comp] += zp[half, comp, pl.ds(WIN - r, 2 * WIN), :]
            return carry

        lax.fori_loop(0, SCANS, step, 0, unroll=True)

    def all_reduce(rnd, probe_now, j):
        rows = piece + (8 if j == 0 else 0)
        n = pl.ds(0, rows)
        copies = []

        def go(new, order=None):
            for i in order or range(len(new)):
                new[i].start()
            copies.extend(new)
            return new

        theirs = pl.ds(pl.multiple_of((1 - core) * HALF + j * CHUNK, CHUNK), CHUNK)
        new = [remote(pg.at[rnd, theirs, :], crb.at[rnd, j], co_s.at[rnd, j], co_r.at[rnd, j], partner)]
        if j == 0:
            new.append(remote(wacc.at[rnd], wcb.at[rnd], co_s.at[rnd, PAIRS], co_r.at[rnd, PAIRS], partner))
        new = go(new)
        yield
        for copy in new:
            copy.wait_recv()
        mine = pl.ds(pl.multiple_of(core * HALF + j * CHUNK, CHUNK), CHUNK)
        hs[rnd, j, :, 0:piece, :] = (pg[rnd, mine, :] + crb[rnd, j]).reshape(X * Y, piece, WIN)
        if j == 0:
            hs[rnd, j, :, piece:, :] = jnp.broadcast_to((wacc[rnd] + wcb[rnd])[None], (X * Y, 8, WIN))
        new = []
        for d in range(1, X * Y):
            device, pq = xy_peer(d)
            new.append(remote(hs.at[rnd, j, pq, n, :], rxb.at[rnd, j, q, n, :], xy_s.at[rnd, j, d], xy_r.at[rnd, j, d], device))
        new = go(new, far_xy)
        rxb[rnd, j, q, 0:rows, :] = hs[rnd, j, q, 0:rows, :]
        yield
        for copy in new:
            copy.wait_recv()
        total = rxb[rnd, j, 0, 0:rows, :]
        for i in range(1, X * Y):
            total = total + rxb[rnd, j, i, 0:rows, :]
        zbuf[rnd, j, z, 0:rows, :] = total
        here = zbuf.at[rnd, j, z, n, :]
        new = go([remote(here, here, z_s.at[rnd, j, d], z_r.at[rnd, j, d], z_peer(d)) for d in range(1, nz)], far_z)
        yield
        for copy in new:
            copy.wait_recv()
        total = zbuf[rnd, j, 0, 0:rows, :]
        for i in range(1, nz):
            total = total + zbuf[rnd, j, i, 0:rows, :]
        if j == 0:
            wcb[rnd] = jnp.broadcast_to(jnp.sum(total[piece:], axis=(0, 1), keepdims=True), (8, WIN))
        scale = PROBE_RELAX * WIN * WIN / wcb[rnd, 0:1, :]
        base = core * HALF + j * CHUNK
        place = pl.ds(pl.multiple_of(base + q * piece, piece), piece)
        pn[rnd, place, :] = probe_now[place, :] + scale * total[:piece]
        here = pn.at[rnd, place, :]
        new = go([remote(here, here, ag_s.at[rnd, j, d], ag_r.at[rnd, j, d], xy_peer(d)[0]) for d in range(1, X * Y)], far_xy)
        yield
        forwards = []
        for dx in (0, 1, 3, 2) if X == 4 else range(X):
            for d in range(dx * Y, (dx + 1) * Y):
                if d:
                    new[d - 1].wait_recv()
            group = ((x + X - dx) % X) * Y * piece
            source = pn.at[rnd, pl.ds(pl.multiple_of(base + group, Y * piece), Y * piece), :]
            forwards += go([remote(source, source, fw_s.at[rnd, j, dx], fw_r.at[rnd, j, dx], partner)])
        yield
        for copy in forwards:
            copy.wait_recv()
        sent.append([(copy, True, True) for copy in copies])
        yield

    out_copies = [
        pltpu.make_async_copy(obj_out, obj_hbm_out, in_s.at[4]),
        pltpu.make_async_copy(pn.at[ROUNDS - 1], probe_hbm_out, in_s.at[5]),
    ]

    def object_exchange(rnd, last):
        place(rnd)
        lrp[rnd, 0], _ = pack(gq[rnd, 0, 0], gq[rnd, 0, 1], low2)
        _, lrp[rnd, 1] = pack(gq[rnd, 1, 0], gq[rnd, 1, 1], low2)
        lr = [
            (remote(lrp.at[rnd, 1], lrb.at[rnd, 0], lr_s.at[rnd, 0], lr_r.at[rnd, 0], (ty, right)), has_right, has_left),
            (remote(lrp.at[rnd, 0], lrb.at[rnd, 1], lr_s.at[rnd, 1], lr_r.at[rnd, 1], (ty, left)), has_left, has_right),
        ]
        start(lr)
        yield
        wait_recv(lr)
        a, b = lrb[rnd, 0], lrb[rnd, 1]
        others = (jnp.where(low2, a, pltpu.roll(b, 64, 1)), jnp.where(low2, pltpu.roll(a, 64, 1), b))
        for comp, other in enumerate(others):
            own = jnp.where(low2, pltpu.roll(gq[rnd, 0, comp], 64, 1), pltpu.roll(gq[rnd, 1, comp], 64, 1))
            mb[rnd, comp] = own + other
        n = 64 if last else 128
        ud = [
            (remote(mb.at[rnd, :, pl.ds(256 - n, n), :], udb.at[rnd, 0, :, pl.ds(0, n), :], ud_s.at[rnd, 0], ud_r.at[rnd, 0], (down, tx)), has_down, has_up),
            (remote(mb.at[rnd, :, pl.ds(0, n), :], udb.at[rnd, 1, :, pl.ds(0, n), :], ud_s.at[rnd, 1], ud_r.at[rnd, 1], (up, tx)), has_up, has_down),
        ]
        start(ud)
        sent.extend([lr, ud])
        yield
        wait_recv(ud)
        if last:
            for comp in range(2):
                add = jnp.concatenate([udb[rnd, 0, comp, 0:64, :], udb[rnd, 1, comp, 0:64, :]], axis=0)
                obj_out[comp] = objm[rnd, comp, 64:192, :] + OBJECT_STEP * (mb[rnd, comp, 64:192, :] + add)
            out_copies[0].start()
            yield
            return
        row = lax.broadcasted_iota(jnp.int32, (WIN, WIN), 0)
        there = ((row >= 64) | has_up, (row < 64) | has_down)
        for comp in range(2):
            for half in range(2):
                rows = slice(half * WIN, (half + 1) * WIN)
                add = mb[rnd, comp, rows, :] + udb[rnd, half, comp]
                objm[rnd + 1, comp, rows, :] = objm[rnd, comp, rows, :] + jnp.where(there[half], OBJECT_STEP * add, 0.0)
        pk[rnd + 1, 0], pk[rnd + 1, 1] = pack(objm[rnd + 1, 0], objm[rnd + 1, 1], low2)
        side = [
            (remote(pk.at[rnd + 1, 1], hlr.at[rnd + 1, 0], halo_s.at[8 + 2 * rnd], halo_r.at[8 + 2 * rnd], (ty, right)), has_right, has_left),
            (remote(pk.at[rnd + 1, 0], hlr.at[rnd + 1, 1], halo_s.at[9 + 2 * rnd], halo_r.at[9 + 2 * rnd], (ty, left)), has_left, has_right),
        ]
        start(side)
        sent.append(side)
        yield
        wait_recv(side)
        yield

    for rnd in range(ROUNDS):
        last = rnd == ROUNDS - 1
        probe_now = probe if rnd == 0 else pn.at[rnd - 1]
        if rnd == 0:
            windows(rnd)
            forward(probe_now, 0)
        forward(probe_now, 1)
        steps = {"0": all_reduce(rnd, probe_now, 0), "1": all_reduce(rnd, probe_now, 1), "o": object_exchange(rnd, last)}

        def do(order):
            for name in order:
                next(steps[name])

        backward(rnd, probe_now, 0, 0, SCANS)
        do("0")
        if MIDDLE:
            backward(rnd, probe_now, 1, 0, 1)
            do(MIDDLE)
            backward(rnd, probe_now, 1, 1, SCANS)
        else:
            backward(rnd, probe_now, 1, 0, SCANS)
        if last:
            do(LAST)
        else:
            do(FIRST)
            windows(rnd + 1)
            forward(pn.at[rnd], 0)
            do("1")
    out_copies[1].start()
    for copies in sent:
        wait_send(copies)
    for copy in out_copies:
        copy.wait()


def deliver(obj, probe, obj_out, probe_out, a, b, in_s, out_s):
    refs = [(obj, a, obj_out)]
    for i in range(4):
        rows = pl.ds(i * HALF // 2, HALF // 2)
        refs.append((probe.at[rows, :], b.at[rows, :], probe_out.at[rows, :]))
    loads = [pltpu.make_async_copy(x, y, in_s.at[i]) for i, (x, y, _) in enumerate(refs)]
    stores = [pltpu.make_async_copy(y, z, out_s.at[i]) for i, (_, y, z) in enumerate(refs)]
    for copy in loads:
        copy.start()
    for load, store in zip(loads, stores):
        load.wait()
        store.start()
    for copy in stores:
        copy.wait()


def per_device(object_field, probe, intensities, positions):
    nq, nz = X * Y, ZH * ZL
    slot = CHUNK // nq + 8
    vmem = lambda *shape, dtype=F32: pltpu.VMEM(shape, dtype)
    dma = lambda *shape: pltpu.SemaphoreType.DMA(shape)
    r = ROUNDS
    hbm = pl.BlockSpec(memory_space=pltpu.MemorySpace.HBM)
    obj, new_probe = pl.pallas_call(
        kernel,
        out_shape=(
            jax.ShapeDtypeStruct((2, WIN, WIN), F32),
            jax.ShapeDtypeStruct((2 * HALF, WIN), F32),
        ),
        in_specs=[hbm, hbm, hbm, pl.BlockSpec(memory_space=pltpu.SMEM), hbm],
        out_specs=(hbm, hbm),
        scratch_shapes=[
            vmem(2, WIN, WIN),
            vmem(2 * HALF, WIN),
            vmem(SCANS, WIN, WIN),
            vmem(4, 256, 256, dtype=BF16),
            vmem(r, 2, 256, 128),
            vmem(r, 2, 256, 128),
            vmem(r, 2, 256, 128),
            vmem(2, 2, 256, 128),
            vmem(2, 2, 384, 128),
            vmem(r, 2, 2, 256, 128),
            vmem(r, 2, 256, 128),
            vmem(r, 2, 256, 128),
            vmem(r, 2, 256, 128),
            vmem(r, 2, 2, 128, 128),
            vmem(SCANS, PAIRS, 256, 256),
            vmem(SCANS, 128, 128),
            vmem(SCANS, 2, 128, 128),
            vmem(SCANS, 2, 128, 128),
            vmem(r, 2 * HALF, 128),
            vmem(r, 8, 128),
            vmem(r, PAIRS, CHUNK, 128),
            vmem(r, 8, 128),
            vmem(r, PAIRS, nq, slot, 128),
            vmem(r, PAIRS, nq, slot, 128),
            vmem(r, PAIRS, nz, slot, 128),
            vmem(r, 2 * HALF, 128),
            dma(6),
            dma(8 + 2 * r), dma(8 + 2 * r),
            dma(r, 2), dma(r, 2),
            dma(r, 2), dma(r, 2),
            dma(r, PAIRS + 1), dma(r, PAIRS + 1),
            dma(r, PAIRS, nq), dma(r, PAIRS, nq),
            dma(r, PAIRS, nz), dma(r, PAIRS, nz),
            dma(r, PAIRS, nq), dma(r, PAIRS, nq),
            dma(r, PAIRS, X), dma(r, PAIRS, X),
        ],
        compiler_params=pltpu.CompilerParams(
            collective_id=0, has_side_effects=True, vmem_limit_bytes=66_000_000
        ),
    )(
        object_field,
        probe.reshape(2 * HALF, WIN),
        intensities.reshape(SCANS, WIN, WIN),
        positions.reshape(SCANS, 2).T,
        jnp.asarray(dft_tables()),
    )
    obj, new_probe = pl.pallas_call(
        deliver,
        out_shape=(
            jax.ShapeDtypeStruct((2, WIN, WIN), F32),
            jax.ShapeDtypeStruct((2 * HALF, WIN), F32),
        ),
        in_specs=[hbm, hbm],
        out_specs=(hbm, hbm),
        scratch_shapes=[vmem(2, WIN, WIN), vmem(2 * HALF, WIN), dma(5), dma(5)],
        compiler_params=pltpu.CompilerParams(vmem_limit_bytes=66_000_000),
    )(obj, new_probe)
    return obj, new_probe.reshape(2, MODES, WIN, WIN)


def solution(mesh):
    placed = (P(None, "ty", "tx"), P(), P("ty", "tx", None, None, None), P("ty", "tx", None, None))
    return jax.shard_map(
        per_device,
        mesh=mesh,
        in_specs=placed,
        out_specs=(P(None, "ty", "tx"), P()),
        check_vma=False,
    )
```

```python
import jax
import jax.numpy as jnp
import ml_dtypes
import numpy as np
from jax import lax
from jax.experimental import pallas as pl
from jax.experimental.pallas import tpu as pltpu
from jax.sharding import PartitionSpec as P

ROUNDS = 2
OBJECT_STEP = 0.1
PROBE_RELAX = 0.5
WIN = 128
MODES = 4
SCANS = 3
PAIRS = MODES // 2
X, Y, ZH, ZL = 4, 4, 2, 4
HALF = MODES * WIN
CHUNK = HALF // PAIRS
MESH = pl.DeviceIdType.MESH
MIDDLE = "0"
FIRST = "1o101o010o10o"
LAST = "1o101o01o0101"
F32, BF16 = jnp.float32, jnp.bfloat16


def dft_tables():
    line = np.arange(WIN)
    angle = (line[:, None] * line[None, :] % WIN) * (2.0 * np.pi / WIN)
    c, s = np.cos(angle) * WIN**-0.5, np.sin(angle) * WIN**-0.5
    a = np.block([[c, -s], [s, c]])
    parts = []
    for m in (a, a.T):
        hi = m.astype(ml_dtypes.bfloat16)
        lo = (m - hi.astype(np.float64)).astype(ml_dtypes.bfloat16)
        parts += [hi, lo]
    return np.stack(parts)


def split(x):
    hi = x.astype(BF16)
    return hi, (x - hi.astype(F32)).astype(BF16)


def mm(a, b):
    return jnp.dot(a, b, preferred_element_type=F32)


def left_mm(tab, i, x):
    hi, lo = split(x)
    return mm(tab[i], hi) + mm(tab[i], lo) + mm(tab[i + 1], hi)


def right_mm(x, tab, i):
    hi, lo = split(x)
    return mm(hi, tab[i]) + mm(lo, tab[i]) + mm(hi, tab[i + 1])


def regroup(t):
    top = jnp.concatenate([t[:WIN, :WIN], t[WIN:, :WIN]], axis=1)
    bottom = jnp.concatenate([t[:WIN, WIN:], t[WIN:, WIN:]], axis=1)
    return jnp.concatenate([top, bottom], axis=0)


def kernel(
    obj_hbm, probe_hbm, inten_hbm, pos, tab_hbm, obj_hbm_out, probe_hbm_out, obj_out,
    probe, inten, tab, objm, hlr, pk, ext, zp, gq, lrp, lrb, mb, udb, uf, pw, win, gs, pg, wacc,
    crb, wcb, hs, rxb, zbuf, pn,
    in_s, halo_s, halo_r, lr_s, lr_r, ud_s, ud_r, co_s, co_r, xy_s, xy_r, z_s, z_r, ag_s, ag_r, fw_s, fw_r,
):
    ty, tx = lax.axis_index("ty"), lax.axis_index("tx")
    nty, ntx = ZH * X, ZL * Y * 2
    zh, x = ty // X, ty % X
    zl, y, core = tx // (2 * Y), (tx // 2) % Y, tx % 2
    z = zh * ZL + zl
    q = x * Y + y
    piece = CHUNK // (X * Y)
    nz = ZH * ZL

    has_up, has_down = ty > 0, ty < nty - 1
    has_left, has_right = tx > 0, tx < ntx - 1
    up, down = (ty + nty - 1) % nty, (ty + 1) % nty
    left, right = (tx + ntx - 1) % ntx, (tx + 1) % ntx
    partner = (ty, tx + 1 - 2 * core)

    def xy_peer(d):
        px, py = (x + d // Y) % X, (y + d % Y) % Y
        return (zh * X + px, zl * 2 * Y + py * 2 + core), px * Y + py

    def z_peer(d):
        pz = (z + d) % nz
        return ((pz // ZL) * X + x, (pz % ZL) * 2 * Y + y * 2 + core)

    ring = lambda d, n: min(d, n - d)
    far_xy = sorted(range(X * Y - 1), key=lambda i: -ring((i + 1) // Y, X) - ring((i + 1) % Y, Y))
    far_z = sorted(range(nz - 1), key=lambda i: -ring(i + 1, nz))

    def remote(src, dst, ssem, rsem, device):
        return pltpu.make_async_remote_copy(
            src_ref=src, dst_ref=dst, send_sem=ssem, recv_sem=rsem, device_id=device, device_id_type=MESH
        )

    loads = [
        pltpu.make_async_copy(obj_hbm, objm.at[0, :, pl.ds(64, WIN), :], in_s.at[0]),
        pltpu.make_async_copy(probe_hbm, probe, in_s.at[1]),
        pltpu.make_async_copy(tab_hbm, tab, in_s.at[2]),
        pltpu.make_async_copy(inten_hbm, inten, in_s.at[3]),
    ]
    for copy in loads:
        copy.start()
    peers = [partner, (ty, left), (ty, right), (up, tx), (down, tx), (up, left), (up, right), (down, left), (down, right)]
    peers += [xy_peer(d)[0] for d in range(1, X * Y)] + [z_peer(d) for d in range(1, nz)]
    barrier = pltpu.get_barrier_semaphore()
    for peer in peers:
        pl.semaphore_signal(barrier, inc=1, device_id=peer, device_id_type=MESH)

    low = lax.broadcasted_iota(jnp.int32, (WIN, WIN), 1) < 64
    lane = lax.broadcasted_iota(jnp.int32, (WIN, WIN), 1)
    low2 = lax.broadcasted_iota(jnp.int32, (2 * WIN, WIN), 1) < 64
    zp[...] = jnp.zeros_like(zp)
    loads[0].wait()

    def pack(re, im, low):
        return jnp.where(low, re, pltpu.roll(im, 64, 1)), jnp.where(low, pltpu.roll(re, 64, 1), im)

    pk[0, 0, 64:192, :], pk[0, 1, 64:192, :] = pack(objm[0, 0, 64:192, :], objm[0, 1, 64:192, :], low)

    @pl.when(jnp.logical_not(has_left))
    def _():
        hlr[:, 0] = jnp.zeros_like(hlr.at[:, 0])
        lrb[:, 0] = jnp.zeros_like(lrb.at[:, 0])

    @pl.when(jnp.logical_not(has_right))
    def _():
        hlr[:, 1] = jnp.zeros_like(hlr.at[:, 1])
        lrb[:, 1] = jnp.zeros_like(lrb.at[:, 1])

    @pl.when(jnp.logical_not(has_up))
    def _():
        hlr[0, :, 0:64, :] = jnp.zeros((2, 64, WIN), F32)
        objm[0, :, 0:64, :] = jnp.zeros((2, 64, WIN), F32)
        udb[:, 0] = jnp.zeros_like(udb.at[:, 0])

    @pl.when(jnp.logical_not(has_down))
    def _():
        hlr[0, :, 192:256, :] = jnp.zeros((2, 64, WIN), F32)
        objm[0, :, 192:256, :] = jnp.zeros((2, 64, WIN), F32)
        udb[:, 1] = jnp.zeros_like(udb.at[:, 1])

    pl.semaphore_wait(barrier, len(peers))

    def start(copies):
        for copy, to, _ in copies:
            @pl.when(to)
            def _():
                copy.start()

    def wait_recv(copies):
        for copy, _, came in copies:
            @pl.when(came)
            def _():
                copy.wait_recv()

    def wait_send(copies):
        for copy, to, _ in copies:
            @pl.when(to)
            def _():
                copy.wait_send()

    top, bottom, mid = pl.ds(64, 64), pl.ds(128, 64), pl.ds(64, 128)
    above, below = pl.ds(0, 64), pl.ds(192, 64)
    halo = [
        (objm.at[0, :, bottom, :], objm.at[0, :, above, :], (down, tx), has_down, has_up),
        (objm.at[0, :, top, :], objm.at[0, :, below, :], (up, tx), has_up, has_down),
        (pk.at[0, 1, mid, :], hlr.at[0, 0, mid, :], (ty, right), has_right, has_left),
        (pk.at[0, 0, mid, :], hlr.at[0, 1, mid, :], (ty, left), has_left, has_right),
        (pk.at[0, 1, bottom, :], hlr.at[0, 0, above, :], (down, right), has_down & has_right, has_up & has_left),
        (pk.at[0, 0, bottom, :], hlr.at[0, 1, above, :], (down, left), has_down & has_left, has_up & has_right),
        (pk.at[0, 1, top, :], hlr.at[0, 0, below, :], (up, right), has_up & has_right, has_down & has_left),
        (pk.at[0, 0, top, :], hlr.at[0, 1, below, :], (up, left), has_up & has_left, has_down & has_right),
    ]
    halo = [(remote(s, d, halo_s.at[i], halo_r.at[i], p), to, came) for i, (s, d, p, to, came) in enumerate(halo)]
    start(halo)
    for copy in loads[1:]:
        copy.wait()
    sent = [halo]
    wait_recv(halo)

    def windows(rnd):
        m_re, m_im = pltpu.roll(objm[rnd, 0], 64, 1), pltpu.roll(objm[rnd, 1], 64, 1)
        fl, fr = hlr[rnd, 0], hlr[rnd, 1]
        ext[0, 0] = jnp.where(low2, fl, m_re)
        ext[0, 1] = jnp.where(low2, pltpu.roll(fl, 64, 1), m_im)
        ext[1, 0] = jnp.where(low2, m_re, pltpu.roll(fr, 64, 1))
        ext[1, 1] = jnp.where(low2, m_im, fr)
        wacc[rnd] = jnp.zeros_like(wacc.at[rnd])
        gq[rnd] = jnp.zeros_like(gq.at[rnd])
        pg[rnd] = jnp.zeros_like(pg.at[rnd])

        def cut(s, carry):
            r, c = pos[0, s], pos[1, s]
            back = (WIN - c) & (WIN - 1)
            first = lane + c < WIN
            w = wacc[rnd]
            for comp in range(2):
                x0 = pltpu.roll(ext[0, comp, pl.ds(r, WIN), :], back, 1)
                x1 = pltpu.roll(ext[1, comp, pl.ds(r, WIN), :], back, 1)
                o = jnp.where(first, x0, x1)
                win[s, comp] = o
                w = w + jnp.sum((o * o).reshape(WIN // 8, 8, WIN), axis=0)
            wacc[rnd] = w
            return carry

        lax.fori_loop(0, SCANS, cut, 0, unroll=True)

    def modes_of(ref, j):
        return [
            (ref[k * WIN : (k + 1) * WIN, :], ref[HALF + k * WIN : HALF + (k + 1) * WIN, :])
            for k in range(2 * j, 2 * j + 2)
        ]

    def forward(probe_now, j):
        def step(s, carry):
            w_re, w_im = win[s, 0], win[s, 1]
            (a_re, a_im), (b_re, b_im) = modes_of(probe_now, j)
            wave_re = jnp.concatenate([a_re * w_re - a_im * w_im, b_re * w_re - b_im * w_im], axis=1)
            wave_im = jnp.concatenate([a_re * w_im + a_im * w_re, b_re * w_im + b_im * w_re], axis=1)
            t = left_mm(tab, 2, jnp.concatenate([wave_re, wave_im], axis=0))
            u = right_mm(regroup(t), tab, 0)
            uf[s, j] = u
            u2 = u * u
            p = (u2[:WIN, :WIN] + u2[:WIN, WIN:]) + (u2[WIN:, :WIN] + u2[WIN:, WIN:])
            if j == 0:
                pw[s] = p
            else:
                p = pw[s] + p
                pw[s] = jnp.sqrt(inten[s]) / jnp.sqrt(jnp.maximum(p, 1.0)) - 1.0
            return carry

        lax.fori_loop(0, SCANS, step, 0, unroll=True)

    def backward(rnd, probe_now, j, lo, hi):
        def step(s, carry):
            f = jnp.concatenate([pw[s], pw[s]], axis=1)
            b = right_mm(uf[s, j] * jnp.concatenate([f, f], axis=0), tab, 2)
            t = left_mm(tab, 0, regroup(b))
            w_re, w_im = win[s, 0], win[s, 1]
            g_re, g_im = (0.0, 0.0) if j == 0 else (gs[s, 0], gs[s, 1])
            for i, (p_re, p_im) in enumerate(modes_of(probe_now, j)):
                k = 2 * j + i
                b_re, b_im = t[:WIN, i * WIN : (i + 1) * WIN], t[WIN:, i * WIN : (i + 1) * WIN]
                g_re = g_re + p_re * b_re + p_im * b_im
                g_im = g_im + p_re * b_im - p_im * b_re
                pg[rnd, k * WIN : (k + 1) * WIN, :] += w_re * b_re + w_im * b_im
                pg[rnd, HALF + k * WIN : HALF + (k + 1) * WIN, :] += w_re * b_im - w_im * b_re
            gs[s, 0], gs[s, 1] = g_re, g_im
            return carry

        lax.fori_loop(lo, hi, step, 0, unroll=True)

    def place(rnd):
        def step(s, carry):
            r, c = pos[0, s], pos[1, s]
            turn = c & (WIN - 1)
            inside = lane >= c
            for comp in range(2):
                g = pltpu.roll(gs[s, comp], turn, 1)
                zp[0, comp, WIN : 2 * WIN, :] = jnp.where(inside, g, 0.0)
                zp[1, comp, WIN : 2 * WIN, :] = jnp.where(inside, 0.0, g)
            for half in range(2):
                for comp in range(2):
                    gq[rnd, half, comp] += zp[half, comp, pl.ds(WIN - r, 2 * WIN), :]
            return carry

        lax.fori_loop(0, SCANS, step, 0, unroll=True)

    def all_reduce(rnd, probe_now, j):
        rows = piece + (8 if j == 0 else 0)
        n = pl.ds(0, rows)
        copies = []

        def go(new, order=None):
            for i in order or range(len(new)):
                new[i].start()
            copies.extend(new)
            return new

        theirs = pl.ds(pl.multiple_of((1 - core) * HALF + j * CHUNK, CHUNK), CHUNK)
        new = [remote(pg.at[rnd, theirs, :], crb.at[rnd, j], co_s.at[rnd, j], co_r.at[rnd, j], partner)]
        if j == 0:
            new.append(remote(wacc.at[rnd], wcb.at[rnd], co_s.at[rnd, PAIRS], co_r.at[rnd, PAIRS], partner))
        new = go(new)
        yield
        for copy in new:
            copy.wait_recv()
        mine = pl.ds(pl.multiple_of(core * HALF + j * CHUNK, CHUNK), CHUNK)
        hs[rnd, j, :, 0:piece, :] = (pg[rnd, mine, :] + crb[rnd, j]).reshape(X * Y, piece, WIN)
        if j == 0:
            hs[rnd, j, :, piece:, :] = jnp.broadcast_to((wacc[rnd] + wcb[rnd])[None], (X * Y, 8, WIN))
        new = []
        for d in range(1, X * Y):
            device, pq = xy_peer(d)
            new.append(remote(hs.at[rnd, j, pq, n, :], rxb.at[rnd, j, q, n, :], xy_s.at[rnd, j, d], xy_r.at[rnd, j, d], device))
        new = go(new, far_xy)
        rxb[rnd, j, q, 0:rows, :] = hs[rnd, j, q, 0:rows, :]
        yield
        for copy in new:
            copy.wait_recv()
        total = rxb[rnd, j, 0, 0:rows, :]
        for i in range(1, X * Y):
            total = total + rxb[rnd, j, i, 0:rows, :]
        zbuf[rnd, j, z, 0:rows, :] = total
        here = zbuf.at[rnd, j, z, n, :]
        new = go([remote(here, here, z_s.at[rnd, j, d], z_r.at[rnd, j, d], z_peer(d)) for d in range(1, nz)], far_z)
        yield
        for copy in new:
            copy.wait_recv()
        total = zbuf[rnd, j, 0, 0:rows, :]
        for i in range(1, nz):
            total = total + zbuf[rnd, j, i, 0:rows, :]
        if j == 0:
            wcb[rnd] = jnp.broadcast_to(jnp.sum(total[piece:], axis=(0, 1), keepdims=True), (8, WIN))
        scale = PROBE_RELAX * WIN * WIN / wcb[rnd, 0:1, :]
        base = core * HALF + j * CHUNK
        place = pl.ds(pl.multiple_of(base + q * piece, piece), piece)
        pn[rnd, place, :] = probe_now[place, :] + scale * total[:piece]
        here = pn.at[rnd, place, :]
        new = go([remote(here, here, ag_s.at[rnd, j, d], ag_r.at[rnd, j, d], xy_peer(d)[0]) for d in range(1, X * Y)], far_xy)
        yield
        forwards = []
        for dx in (0, 1, 3, 2) if X == 4 else range(X):
            for d in range(dx * Y, (dx + 1) * Y):
                if d:
                    new[d - 1].wait_recv()
            group = ((x + X - dx) % X) * Y * piece
            source = pn.at[rnd, pl.ds(pl.multiple_of(base + group, Y * piece), Y * piece), :]
            forwards += go([remote(source, source, fw_s.at[rnd, j, dx], fw_r.at[rnd, j, dx], partner)])
        yield
        for copy in forwards:
            copy.wait_recv()
        sent.append([(copy, True, True) for copy in copies])
        yield

    out_copies = [
        pltpu.make_async_copy(obj_out, obj_hbm_out, in_s.at[4]),
    ]
    for i in range(2 * PAIRS):
        rows = pl.ds((i % 2) * HALF + (i // 2) * CHUNK, CHUNK)
        out_copies.append(pltpu.make_async_copy(pn.at[ROUNDS - 1, rows, :], probe_hbm_out.at[rows, :], in_s.at[5 + i]))

    def object_exchange(rnd, last):
        place(rnd)
        lrp[rnd, 0], _ = pack(gq[rnd, 0, 0], gq[rnd, 0, 1], low2)
        _, lrp[rnd, 1] = pack(gq[rnd, 1, 0], gq[rnd, 1, 1], low2)
        lr = [
            (remote(lrp.at[rnd, 1], lrb.at[rnd, 0], lr_s.at[rnd, 0], lr_r.at[rnd, 0], (ty, right)), has_right, has_left),
            (remote(lrp.at[rnd, 0], lrb.at[rnd, 1], lr_s.at[rnd, 1], lr_r.at[rnd, 1], (ty, left)), has_left, has_right),
        ]
        start(lr)
        yield
        wait_recv(lr)
        a, b = lrb[rnd, 0], lrb[rnd, 1]
        others = (jnp.where(low2, a, pltpu.roll(b, 64, 1)), jnp.where(low2, pltpu.roll(a, 64, 1), b))
        for comp, other in enumerate(others):
            own = jnp.where(low2, pltpu.roll(gq[rnd, 0, comp], 64, 1), pltpu.roll(gq[rnd, 1, comp], 64, 1))
            mb[rnd, comp] = own + other
        n = 64 if last else 128
        ud = [
            (remote(mb.at[rnd, :, pl.ds(256 - n, n), :], udb.at[rnd, 0, :, pl.ds(0, n), :], ud_s.at[rnd, 0], ud_r.at[rnd, 0], (down, tx)), has_down, has_up),
            (remote(mb.at[rnd, :, pl.ds(0, n), :], udb.at[rnd, 1, :, pl.ds(0, n), :], ud_s.at[rnd, 1], ud_r.at[rnd, 1], (up, tx)), has_up, has_down),
        ]
        start(ud)
        sent.extend([lr, ud])
        yield
        wait_recv(ud)
        if last:
            for comp in range(2):
                add = jnp.concatenate([udb[rnd, 0, comp, 0:64, :], udb[rnd, 1, comp, 0:64, :]], axis=0)
                obj_out[comp] = objm[rnd, comp, 64:192, :] + OBJECT_STEP * (mb[rnd, comp, 64:192, :] + add)
            out_copies[0].start()
            yield
            return
        row = lax.broadcasted_iota(jnp.int32, (WIN, WIN), 0)
        there = ((row >= 64) | has_up, (row < 64) | has_down)
        for comp in range(2):
            for half in range(2):
                rows = slice(half * WIN, (half + 1) * WIN)
                add = mb[rnd, comp, rows, :] + udb[rnd, half, comp]
                objm[rnd + 1, comp, rows, :] = objm[rnd, comp, rows, :] + jnp.where(there[half], OBJECT_STEP * add, 0.0)
        pk[rnd + 1, 0], pk[rnd + 1, 1] = pack(objm[rnd + 1, 0], objm[rnd + 1, 1], low2)
        side = [
            (remote(pk.at[rnd + 1, 1], hlr.at[rnd + 1, 0], halo_s.at[8 + 2 * rnd], halo_r.at[8 + 2 * rnd], (ty, right)), has_right, has_left),
            (remote(pk.at[rnd + 1, 0], hlr.at[rnd + 1, 1], halo_s.at[9 + 2 * rnd], halo_r.at[9 + 2 * rnd], (ty, left)), has_left, has_right),
        ]
        start(side)
        sent.append(side)
        yield
        wait_recv(side)
        yield

    for rnd in range(ROUNDS):
        last = rnd == ROUNDS - 1
        probe_now = probe if rnd == 0 else pn.at[rnd - 1]
        if rnd == 0:
            windows(rnd)
            forward(probe_now, 0)
        forward(probe_now, 1)
        steps = {"0": all_reduce(rnd, probe_now, 0), "1": all_reduce(rnd, probe_now, 1), "o": object_exchange(rnd, last)}

        def do(order):
            for name in order:
                next(steps[name])

        backward(rnd, probe_now, 0, 0, SCANS)
        do("0")
        if MIDDLE:
            backward(rnd, probe_now, 1, 0, 1)
            do(MIDDLE)
            backward(rnd, probe_now, 1, 1, SCANS)
        else:
            backward(rnd, probe_now, 1, 0, SCANS)
        if last:
            do(LAST[:-1])
            out_copies[1].start()
            out_copies[2].start()
            do(LAST[-1])
        else:
            do(FIRST)
            windows(rnd + 1)
            forward(pn.at[rnd], 0)
            do("1")
    out_copies[3].start()
    out_copies[4].start()
    for copies in sent:
        wait_send(copies)
    for copy in out_copies:
        copy.wait()


def deliver(obj, probe, obj_out, probe_out, a, b, in_s, out_s):
    refs = [(obj, a, obj_out)]
    for i in range(4):
        rows = pl.ds(i * HALF // 2, HALF // 2)
        refs.append((probe.at[rows, :], b.at[rows, :], probe_out.at[rows, :]))
    loads = [pltpu.make_async_copy(x, y, in_s.at[i]) for i, (x, y, _) in enumerate(refs)]
    stores = [pltpu.make_async_copy(y, z, out_s.at[i]) for i, (_, y, z) in enumerate(refs)]
    for copy in loads:
        copy.start()
    for load, store in zip(loads, stores):
        load.wait()
        store.start()
    for copy in stores:
        copy.wait()


def per_device(object_field, probe, intensities, positions):
    nq, nz = X * Y, ZH * ZL
    slot = CHUNK // nq + 8
    vmem = lambda *shape, dtype=F32: pltpu.VMEM(shape, dtype)
    dma = lambda *shape: pltpu.SemaphoreType.DMA(shape)
    r = ROUNDS
    hbm = pl.BlockSpec(memory_space=pltpu.MemorySpace.HBM)
    obj, new_probe = pl.pallas_call(
        kernel,
        out_shape=(
            jax.ShapeDtypeStruct((2, WIN, WIN), F32),
            jax.ShapeDtypeStruct((2 * HALF, WIN), F32),
        ),
        in_specs=[hbm, hbm, hbm, pl.BlockSpec(memory_space=pltpu.SMEM), hbm],
        out_specs=(hbm, hbm),
        scratch_shapes=[
            vmem(2, WIN, WIN),
            vmem(2 * HALF, WIN),
            vmem(SCANS, WIN, WIN),
            vmem(4, 256, 256, dtype=BF16),
            vmem(r, 2, 256, 128),
            vmem(r, 2, 256, 128),
            vmem(r, 2, 256, 128),
            vmem(2, 2, 256, 128),
            vmem(2, 2, 384, 128),
            vmem(r, 2, 2, 256, 128),
            vmem(r, 2, 256, 128),
            vmem(r, 2, 256, 128),
            vmem(r, 2, 256, 128),
            vmem(r, 2, 2, 128, 128),
            vmem(SCANS, PAIRS, 256, 256),
            vmem(SCANS, 128, 128),
            vmem(SCANS, 2, 128, 128),
            vmem(SCANS, 2, 128, 128),
            vmem(r, 2 * HALF, 128),
            vmem(r, 8, 128),
            vmem(r, PAIRS, CHUNK, 128),
            vmem(r, 8, 128),
            vmem(r, PAIRS, nq, slot, 128),
            vmem(r, PAIRS, nq, slot, 128),
            vmem(r, PAIRS, nz, slot, 128),
            vmem(r, 2 * HALF, 128),
            dma(5 + 2 * PAIRS),
            dma(8 + 2 * r), dma(8 + 2 * r),
            dma(r, 2), dma(r, 2),
            dma(r, 2), dma(r, 2),
            dma(r, PAIRS + 1), dma(r, PAIRS + 1),
            dma(r, PAIRS, nq), dma(r, PAIRS, nq),
            dma(r, PAIRS, nz), dma(r, PAIRS, nz),
            dma(r, PAIRS, nq), dma(r, PAIRS, nq),
            dma(r, PAIRS, X), dma(r, PAIRS, X),
        ],
        compiler_params=pltpu.CompilerParams(
            collective_id=0, has_side_effects=True, vmem_limit_bytes=66_000_000
        ),
    )(
        object_field,
        probe.reshape(2 * HALF, WIN),
        intensities.reshape(SCANS, WIN, WIN),
        positions.reshape(SCANS, 2).T,
        jnp.asarray(dft_tables()),
    )
    obj, new_probe = pl.pallas_call(
        deliver,
        out_shape=(
            jax.ShapeDtypeStruct((2, WIN, WIN), F32),
            jax.ShapeDtypeStruct((2 * HALF, WIN), F32),
        ),
        in_specs=[hbm, hbm],
        out_specs=(hbm, hbm),
        scratch_shapes=[vmem(2, WIN, WIN), vmem(2 * HALF, WIN), dma(5), dma(5)],
        compiler_params=pltpu.CompilerParams(vmem_limit_bytes=66_000_000),
    )(obj, new_probe)
    return obj, new_probe.reshape(2, MODES, WIN, WIN)


def solution(mesh):
    placed = (P(None, "ty", "tx"), P(), P("ty", "tx", None, None, None), P("ty", "tx", None, None))
    return jax.shard_map(
        per_device,
        mesh=mesh,
        in_specs=placed,
        out_specs=(P(None, "ty", "tx"), P()),
        check_vma=False,
    )
```
